256 devices in a mesh: slab: 16 (over y, x_hi, core), grp: 16 (over x_lo, z).
Axes of the slice: x: 4 (x_hi: 2, x_lo: 2; x = x_hi * 2 + x_lo), y: 4, z: 8, core: 2. Of those that a mesh axis runs over, the one named last changes fastest.
Arguments:
- cloud_states: float32 [2, 64, 4, 128, 1024], P(None, 'grp', None, 'slab'), may hold values from -6 to 6
- cloud_shift: int32 [2], replicated, may hold values from 9 to 15, as said below
- boost_wave: int32 [2], replicated, may hold values from -6 to 6, as said below
Outputs:
- evolved: float32 [2, 64, 4, 128, 1024], P(None, 'grp', None, 'slab')
The draws below stay inside these ranges and needn't reach their ends.
Inputs may be any that keep to these rules, and one draw needn't show every extreme that they name: `cloud_shift`: one of the two entries equals 15. `boost_wave`: the first entry is 6; the second is negative.
All inputs are finite; a program needn't handle non-finite values.
Results may differ from the reference program's by a relative error of at most 0.00002.
Values sent between devices are 32-bit elements; how exact they have to be, the bound alone decides.
A program may use at most 64 MiB of HBM per device.

```python
import math
import jax
import jax.numpy as jnp
from jax import lax

NY = 32
CZ = 8
NXY = 1024
NZ = 128
S = 64


def draw_cloud_shift(key, part):
    key_other = jax.random.fold_in(key, 11)
    key_which = jax.random.fold_in(key, 12)
    other_shift = jax.random.randint(key_other, (), CZ + 1, 2 * CZ, dtype=jnp.int32)
    which_first = jax.random.randint(key_which, (), 0, 2, dtype=jnp.int32)
    largest_shift = jnp.full((), 2 * CZ - 1, dtype=jnp.int32)
    return jnp.where(which_first == 0, jnp.stack([largest_shift, other_shift]), jnp.stack([other_shift, largest_shift])).astype(jnp.int32)


def draw_boost_wave(key, part):
    key_second = jax.random.fold_in(key, 21)
    second_wave = -jax.random.randint(key_second, (), 1, 7, dtype=jnp.int32)
    first_wave = jnp.full((), 6, dtype=jnp.int32)
    return jnp.stack([first_wave, second_wave]).astype(jnp.int32)


def levels(own_key, dims, shards, least, high):
    loudness, own = 1.0, jax.random.fold_in(own_key, 6)
    for dim, shards_of in shards:
        steps = jnp.exp(jax.random.uniform(jax.random.fold_in(own, dim), (shards_of,), jnp.float32, least / len(shards), high / len(shards)))
        loudness = loudness * jnp.repeat(steps, dims[dim] // shards_of).reshape([-1 if axis == dim else 1 for axis in range(len(dims))])
    return loudness


def scatter_about(key, extent, scale, bound, pieces=(), held_as=jnp.bfloat16):
    array = jax.random.normal(key, extent, jnp.float32) * scale
    if len(pieces) > 0:
        array = levels(key, extent, pieces, -0.22, 0.18) * array
    return jnp.clip(array, min=-bound, max=bound).astype(held_as)


def setup_inputs(seed: int = 0) -> dict:
    streams_of = jax.random.split(jax.random.key(seed), 4)
    cloud_states = scatter_about(streams_of[0], (2, S, 4, NZ, NXY), 1.0, 6.0, ((1, 16), (3, 16)), jnp.float32)
    cloud_shift = draw_cloud_shift(jax.random.fold_in(streams_of[3], 71), 0)
    boost_wave = draw_boost_wave(jax.random.fold_in(streams_of[3], 71), 0)
    return {"cloud_states": cloud_states, "cloud_shift": cloud_shift, "boost_wave": boost_wave}


stencil = (-49.0 / 18.0, 1.5, -0.15, 1.0 / 90.0)
coupling = 3.0
xi_factor = 1.2
chemical = 1.0
time_step = 0.1


def transverse(volume, row_width):
    cell_count = volume.shape[-1]
    column = lax.broadcasted_iota(jnp.int32, (cell_count,), 0) % row_width
    pad_spec = [(0, 0)] * (volume.ndim - 1) + [(3 * row_width, 3 * row_width)]
    padded = jnp.pad(volume, pad_spec)
    running = 2.0 * stencil[0] * volume
    base = 3 * row_width
    for offset in range(1, 4):
        for signed in (offset, -offset):
            across_rows = padded[..., base + signed * row_width: base + signed * row_width + cell_count]
            across_columns = padded[..., base + signed: base + signed + cell_count]
            inside = ((column + signed >= 0) & (column + signed < row_width)).astype(jnp.float32)
            running = running + stencil[offset] * (across_rows + across_columns * inside)
    return running


def along_depth(extended, planes):
    running = stencil[0] * extended[..., 3:3 + planes, :]
    for offset in range(1, 4):
        for signed in (offset, -offset):
            running = running + stencil[offset] * extended[..., 3 + signed:3 + signed + planes, :]
    return running


def laplacian(single):
    padded = jnp.pad(single, ((0, 0), (3, 3), (0, 0)), mode="wrap")
    return along_depth(padded, single.shape[1]) + transverse(single, NY)


def fields_of(totals):
    potential = xi_factor * jnp.square(jnp.cbrt(totals[0])) - chemical
    return jnp.stack([potential, -coupling * totals[1], -coupling * totals[2]])


def potentials(states):
    particle_real = states[:, 0]
    particle_imag = states[:, 1]
    hole_real = states[:, 2]
    hole_imag = states[:, 3]
    density = jnp.sum(hole_real * hole_real + hole_imag * hole_imag, axis=0) / S
    pair_real = jnp.sum(particle_real * hole_real + particle_imag * hole_imag, axis=0) / S
    pair_imag = jnp.sum(particle_imag * hole_real - particle_real * hole_imag, axis=0) / S
    return fields_of(jnp.stack([density, pair_real, pair_imag]))


def hamiltonian(single, fields):
    kinetic = -0.5 * laplacian(single)
    potential = fields[0]
    gap_real = fields[1]
    gap_imag = fields[2]
    particle_real, particle_imag, hole_real, hole_imag = single[0], single[1], single[2], single[3]
    out_pr = kinetic[0] + potential * particle_real + gap_real * hole_real - gap_imag * hole_imag
    out_pi = kinetic[1] + potential * particle_imag + gap_real * hole_imag + gap_imag * hole_real
    out_hr = gap_real * particle_real + gap_imag * particle_imag - kinetic[2] - potential * hole_real
    out_hi = gap_real * particle_imag - gap_imag * particle_real - kinetic[3] - potential * hole_imag
    return jnp.stack([out_pr, out_pi, out_hr, out_hi])


def advance(single, change, factor):
    return jnp.stack([single[0] + factor * change[1], single[1] - factor * change[0],
                      single[2] + factor * change[3], single[3] - factor * change[2]])


def reference(cloud_states, cloud_shift, boost_wave):
    planes = jnp.arange(NZ, dtype=jnp.int32)
    source_first = jnp.mod(planes - cloud_shift[0], NZ).astype(jnp.int32)
    source_second = jnp.mod(planes + cloud_shift[1], NZ).astype(jnp.int32)
    first_cloud = jnp.take(cloud_states[0], source_first, axis=2)
    second_cloud = jnp.take(cloud_states[1], source_second, axis=2)
    placed = jnp.stack([first_cloud, second_cloud])
    phase_index = jnp.mod(boost_wave[:, None] * planes[None, :], NZ)
    phases = (2.0 * math.pi / NZ) * phase_index.astype(jnp.float32)
    cosine_table = jnp.cos(phases)[:, None, :, None]
    sine_table = jnp.sin(phases)[:, None, :, None]
    particle_real = placed[:, :, 0]
    particle_imag = placed[:, :, 1]
    hole_real = placed[:, :, 2]
    hole_imag = placed[:, :, 3]
    boosted = jnp.stack([particle_real * cosine_table - particle_imag * sine_table,
                         particle_real * sine_table + particle_imag * cosine_table,
                         hole_real * cosine_table + hole_imag * sine_table,
                         hole_imag * cosine_table - hole_real * sine_table], axis=2)
    flat_states = boosted.reshape(2 * S, 4, NZ, NXY)
    fields_now = potentials(flat_states)

    def predict_one(single):
        return advance(single, hamiltonian(single, fields_now), time_step)

    predicted = lax.map(predict_one, flat_states)
    fields_next = potentials(predicted)

    def correct_one(couple):
        change = hamiltonian(couple[0], fields_now) + hamiltonian(couple[1], fields_next)
        return advance(couple[0], change, time_step / 2.0)

    evolved = lax.map(correct_one, (flat_states, predicted))
    return evolved.reshape(2, S, 4, NZ, NXY)
```

```python
import functools
import math

import jax
import jax.numpy as jnp
import numpy as np
from jax import lax
from jax.experimental import pallas as pl
from jax.experimental.pallas import tpu as pltpu
from jax.sharding import PartitionSpec as P

MESH = pl.DeviceIdType.MESH
W = (-49.0 / 18.0, 1.5, -0.15, 1.0 / 90.0)
DT = 0.1
NZ = 128
STATES = 64
ONE, THREE, TWO, OWN = 0, 1, 2, 3
ORDER = ((THREE, TWO, ONE, OWN), (OWN, ONE, TWO, THREE))


def stencil_tables(scale):
    lane = lax.broadcasted_iota(jnp.int32, (8, 128), 1)
    sub = lax.broadcasted_iota(jnp.int32, (8, 128), 0)
    y = lane % 32
    w = [scale * v for v in W]
    cy = {}
    for s in (1, -1, 2, -2, 3, -3):
        cy[s] = jnp.where((y + s >= 0) & (y + s < 32), w[abs(s)], 0.0)
    m32 = jnp.where(lane >= 32, w[1], w[3])
    m96 = jnp.where(lane < 96, w[1], w[3])
    up = [jnp.where((lane < 32 * j) & (sub < 7), w[j], 0.0) for j in (1, 2, 3)]
    down = [jnp.where((lane >= 128 - 32 * j) & (sub > 0), w[j], 0.0) for j in (1, 2, 3)]
    return w, cy, m32, m96, up, down


def laplacian(tables, ref, vol, row):
    w, cy, m32, m96, up, down = tables

    def plane(d):
        return ref[vol, pl.ds(pl.multiple_of(row + 8 * d, 8), 8), :]

    f = plane(0)
    t = (3.0 * w[0]) * f
    for j in (1, 2, 3):
        t = t + w[j] * (plane(-j) + plane(j))
    for s in (1, -1, 2, -2, 3, -3):
        t = t + cy[s] * pltpu.roll(f, (-s) % 128, 1)
    r32, r64, r96 = (pltpu.roll(f, 32 * j, 1) for j in (1, 2, 3))
    t = t + m32 * r32 + w[2] * r64 + m96 * r96
    above = up[0] * r32 + up[1] * r64 + up[2] * r96
    below = down[0] * r96 + down[1] * r64 + down[2] * r32
    t = t + pltpu.roll(above, 1, 0) + pltpu.roll(below, 7, 0)
    return f, t


def two_thirds(n):
    y = jnp.exp(jnp.log(jnp.maximum(n, 1e-30)) * (1.0 / 3.0))
    y = y - (y * y * y - n) / (3.0 * y * y)
    return y * y


def kernel(shift_ref, boost_ref, cos_ref, sin_ref, x_ref, o_ref,
           r_buf, e_buf, b_buf, p_buf, d1, rs1, t1, s1, sel1, ag1, f0, acc, d2, rs2, t2, ag2,
           x_sem, slab_send, slab_recv, rs1_send, rs1_recv, s1_send, s1_recv, ag1_send, ag1_recv,
           rs2_send, rs2_recv, ag2_send, ag2_recv, halo_send, halo_recv):
    slabs = lax.axis_size("slab")
    groups = lax.axis_size("grp")
    i = lax.axis_index("slab")
    g = lax.axis_index("grp")
    core = lax.rem(i, 2)
    mate = i + 1 - 2 * core

    def slab(d):
        return (lax.rem(i + d + slabs, slabs), g)

    def peer(k):
        return (i, lax.rem(g + k, groups))

    def own_copy(c):
        return pltpu.make_async_copy(x_ref.at[c], r_buf.at[OWN, c], x_sem.at[c])

    own_copy(0).start()
    own_copy(1).start()

    barrier = pltpu.get_barrier_semaphore()
    for d in (1, -1, 2, -2, 3, -3):
        pl.semaphore_signal(barrier, inc=1, device_id=slab(d), device_id_type=MESH)

    def greet(k, _):
        pl.semaphore_signal(barrier, inc=1, device_id=peer(k), device_id_type=MESH)
        return 0

    lax.fori_loop(1, groups, greet, 0)

    for c in range(2):
        own_copy(c).wait()

        def terms(j, _):
            lanes = pl.ds(pl.multiple_of(j * 128, 128), 128)
            n = kr = ki = None
            for s in range(4):
                ur, ui, vr, vi = (r_buf[OWN, c, s, k, :, lanes] for k in range(4))
                a = vr * vr + vi * vi
                b = ur * vr + ui * vi
                e = ui * vr - ur * vi
                n, kr, ki = (a, b, e) if s == 0 else (n + a, kr + b, ki + e)
            for q, v in enumerate((n, kr, ki)):
                d1[pl.ds(c * 192 + q * 8 + j, 8, stride=24), :] = v
            return 0

        lax.fori_loop(0, 8, terms, 0)

    pl.semaphore_wait(barrier, 6 + groups - 1)

    def rows24(o):
        return pl.ds(pl.multiple_of(o * 24, 8), 24)

    def rs1_copy(k):
        o = lax.rem(g + k, groups)
        return pltpu.make_async_remote_copy(
            src_ref=d1.at[rows24(o)], dst_ref=rs1.at[g], send_sem=rs1_send.at[o], recv_sem=rs1_recv.at[g],
            device_id=peer(k), device_id_type=MESH)

    def start(make):
        def body(k, _):
            make(k).start()
            return 0
        lax.fori_loop(1, groups, body, 0)

    def wait_send(make):
        def body(k, _):
            make(k).wait_send()
            return 0
        lax.fori_loop(1, groups, body, 0)

    def wait_recv(buf, sem):
        def body(k, _):
            o = lax.rem(g + k, groups)
            pltpu.make_async_copy(buf.at[o], buf.at[o], sem.at[o]).wait()
            return 0
        lax.fori_loop(1, groups, body, 0)

    start(rs1_copy)
    rs1[g] = d1[rows24(g), :]

    def far_copy(c, s):
        to = 2 - 4 * c
        return pltpu.make_async_remote_copy(
            src_ref=r_buf.at[OWN, c, s], dst_ref=r_buf.at[TWO, c, s],
            send_sem=slab_send.at[TWO, c, s], recv_sem=slab_recv.at[TWO, c, s],
            device_id=slab(to), device_id_type=MESH)

    def near_copy(s):
        return pltpu.make_async_remote_copy(
            src_ref=r_buf.at[OWN, core, s], dst_ref=r_buf.at[ONE, core, s],
            send_sem=slab_send.at[ONE, core, s], recv_sem=slab_recv.at[ONE, core, s],
            device_id=(mate, g), device_id_type=MESH)

    def third_copy(s):
        return pltpu.make_async_remote_copy(
            src_ref=r_buf.at[OWN, 1 - core, s], dst_ref=r_buf.at[THREE, 1 - core, s],
            send_sem=slab_send.at[THREE, 1 - core, s], recv_sem=slab_recv.at[THREE, 1 - core, s],
            device_id=slab(6 * core - 3), device_id_type=MESH)

    def forward_copy(c, s):
        slot = 1 - (c - core) * (c - core)
        return pltpu.make_async_remote_copy(
            src_ref=r_buf.at[TWO, c, s], dst_ref=r_buf.at[slot, c, s],
            send_sem=slab_send.at[slot, c, s], recv_sem=slab_recv.at[slot, c, s],
            device_id=(mate, g), device_id_type=MESH)

    def start_moves(s, _):
        far_copy(0, s).start()
        far_copy(1, s).start()
        near_copy(s).start()
        third_copy(s).start()
        return 0

    lax.fori_loop(0, 4, start_moves, 0)

    wait_recv(rs1, rs1_recv)

    def add24(k, total):
        return total + rs1[k]

    t1[...] = lax.fori_loop(1, groups, add24, rs1[0])
    cloud = g // 8
    plane_own = lax.rem(g, 8)
    way = 1 - 2 * cloud

    def s1_copy(d):
        return pltpu.make_async_remote_copy(
            src_ref=t1, dst_ref=s1.at[d - 1], send_sem=s1_send.at[d - 1], recv_sem=s1_recv.at[d - 1],
            device_id=slab(way * d), device_id_type=MESH)

    s1_copy(1).start()
    s1_copy(2).start()
    s1_copy(1).wait()
    s1_copy(2).wait()
    r0 = shift_ref[0] - 8
    r1 = shift_ref[1] - 8
    steps = plane_own * way + 7 * cloud + shift_ref[cloud] - 8
    sel1[...] = s1[(steps >> 3) & 1]

    def ag1_copy(k):
        o = lax.rem(g + k, groups)
        return pltpu.make_async_remote_copy(
            src_ref=sel1, dst_ref=ag1.at[g], send_sem=ag1_send.at[o], recv_sem=ag1_recv.at[g],
            device_id=peer(k), device_id_type=MESH)

    start(ag1_copy)
    ag1[g] = sel1[...]
    acc[...] = jnp.zeros_like(acc)
    wait_recv(ag1, ag1_recv)

    def fields_now(p, _):
        z = 8 * i + p
        n = kr = ki = None
        for c in range(2):
            src = 8 * c + ((p - r0 if c == 0 else p + r1) & 7)
            index = (2 * boost_ref[c] * z) & (NZ - 1)
            cos, sin = cos_ref[index], sin_ref[index]
            a, b, e = ag1[src, 0:8, :], ag1[src, 8:16, :], ag1[src, 16:24, :]
            b, e = b * cos - e * sin, b * sin + e * cos
            n, kr, ki = (a, b, e) if c == 0 else (n + a, kr + b, ki + e)
        rows = pl.multiple_of(p * 24, 8)
        f0[pl.ds(rows, 8), :] = DT * (1.2 * two_thirds(n * (1.0 / STATES)) - 1.0)
        f0[pl.ds(rows + 8, 8), :] = kr * (-3.0 * DT / STATES)
        f0[pl.ds(rows + 16, 8), :] = ki * (-3.0 * DT / STATES)
        return 0

    lax.fori_loop(0, 8, fields_now, 0)

    tables = stencil_tables(0.5 * DT)
    e_planes = e_buf.reshape(2, 4, 32, 8, 128)

    def state_step(s, _):
        for c in range(2):
            pltpu.make_async_copy(r_buf.at[TWO, c, s], r_buf.at[TWO, c, s], slab_recv.at[TWO, c, s]).wait()
            forward_copy(c, s).start()
        for c in range(2):
            for slot in (ONE, THREE):
                pltpu.make_async_copy(r_buf.at[slot, c, s], r_buf.at[slot, c, s], slab_recv.at[slot, c, s]).wait()
            order = ORDER[c]
            for k in range(4):
                for j in range(8):
                    lanes = slice(128 * j, 128 * j + 128)
                    e_buf[c, k, pl.ds(6 * 8 + j, 2, stride=8), :] = r_buf[order[0], c, s, k, 6:8, lanes]
                    e_buf[c, k, pl.ds(8 * 8 + j, 8, stride=8), :] = r_buf[order[1], c, s, k, :, lanes]
                    e_buf[c, k, pl.ds(16 * 8 + j, 8, stride=8), :] = r_buf[order[2], c, s, k, :, lanes]
                    e_buf[c, k, pl.ds(24 * 8 + j, 2, stride=8), :] = r_buf[order[3], c, s, k, 0:2, lanes]
            vol = (c * 4 + s) * 4
            base = 13 - r0 if c == 0 else 5 + r1

            def boost(q, _):
                index = (boost_ref[c] * (8 * i + q - 3)) & (NZ - 1)
                cos, sin = cos_ref[index], sin_ref[index]
                ur, ui, vr, vi = (e_planes[c, k, (base + q) & 31] for k in range(4))
                to = pl.ds(pl.multiple_of(q * 8, 8), 8)
                b_buf[vol, to, :] = ur * cos - ui * sin
                b_buf[vol + 1, to, :] = ur * sin + ui * cos
                b_buf[vol + 2, to, :] = vr * cos + vi * sin
                b_buf[vol + 3, to, :] = vi * cos - vr * sin
                return 0

            lax.fori_loop(0, 14, boost, 0)

            def predict(p, _):
                row = pl.multiple_of((p + 3) * 8, 8)
                rows = pl.multiple_of(p * 24, 8)
                pot, dr, di = (f0[pl.ds(rows + 8 * q, 8), :] for q in range(3))
                ur, lur = laplacian(tables, b_buf, vol, row)
                ui, lui = laplacian(tables, b_buf, vol + 1, row)
                vr, lvr = laplacian(tables, b_buf, vol + 2, row)
                vi, lvi = laplacian(tables, b_buf, vol + 3, row)
                pur = ur - lui + (pot * ui + dr * vi + di * vr)
                pui = ui + lur - (pot * ur + dr * vr - di * vi)
                pvr = vr + lvi + (dr * ui - di * ur - pot * vi)
                pvi = vi - lvr - (dr * ur + di * ui - pot * vr)
                at = pl.ds(row, 8)
                p_buf[vol, at, :] = pur
                p_buf[vol + 1, at, :] = pui
                p_buf[vol + 2, at, :] = pvr
                p_buf[vol + 3, at, :] = pvi
                acc[pl.ds(rows, 8), :] += pvr * pvr + pvi * pvi
                acc[pl.ds(rows + 8, 8), :] += pur * pvr + pui * pvi
                acc[pl.ds(rows + 16, 8), :] += pui * pvr - pur * pvi
                return 0

            lax.fori_loop(0, 8, predict, 0)
        return 0

    lax.fori_loop(0, 4, state_step, 0)

    for p in range(8):
        for q in range(3):
            v = acc[p * 24 + q * 8:p * 24 + q * 8 + 8, :]
            d2[p, q] = v[0:4]
            d2[8 + p, q] = v[4:8]

    def rs2_copy(k):
        o = lax.rem(g + k, groups)
        return pltpu.make_async_remote_copy(
            src_ref=d2.at[o], dst_ref=rs2.at[g], send_sem=rs2_send.at[o], recv_sem=rs2_recv.at[g],
            device_id=peer(k), device_id_type=MESH)

    start(rs2_copy)

    def halo_copy(d):
        src = pl.ds(24, 24) if d == 0 else pl.ds(64, 24)
        dst = pl.ds(88, 24) if d == 0 else pl.ds(0, 24)
        return pltpu.make_async_remote_copy(
            src_ref=p_buf.at[:, src], dst_ref=p_buf.at[:, dst], send_sem=halo_send.at[d], recv_sem=halo_recv.at[d],
            device_id=slab(2 * d - 1), device_id_type=MESH)

    halo_copy(0).start()
    halo_copy(1).start()
    rs2[g] = d2[g]
    wait_recv(rs2, rs2_recv)

    def add4(k, total):
        return tuple(total[q] + rs2[k, q] for q in range(3))

    n, kr, ki = lax.fori_loop(1, groups, add4, tuple(rs2[0, q] for q in range(3)))
    t2[0] = DT * (1.2 * two_thirds(n * (1.0 / STATES)) - 1.0)
    t2[1] = kr * (-3.0 * DT / STATES)
    t2[2] = ki * (-3.0 * DT / STATES)

    def ag2_copy(k):
        o = lax.rem(g + k, groups)
        return pltpu.make_async_remote_copy(
            src_ref=t2, dst_ref=ag2.at[g], send_sem=ag2_send.at[o], recv_sem=ag2_recv.at[g],
            device_id=peer(k), device_id_type=MESH)

    start(ag2_copy)
    ag2[g] = t2[...]

    halo_copy(0).wait_recv()
    halo_copy(1).wait_recv()

    def kinetic(m, _):
        vol = (m // 8) * 4
        row = pl.multiple_of((lax.rem(m, 8) + 3) * 8, 8)
        at = pl.ds(row, 8)
        ur, lur = laplacian(tables, p_buf, vol, row)
        ui, lui = laplacian(tables, p_buf, vol + 1, row)
        vr, lvr = laplacian(tables, p_buf, vol + 2, row)
        vi, lvi = laplacian(tables, p_buf, vol + 3, row)
        b_buf[vol, at, :] += ur - lui
        b_buf[vol + 1, at, :] += ui + lur
        b_buf[vol + 2, at, :] += vr + lvi
        b_buf[vol + 3, at, :] += vi - lvr
        return 0

    lax.fori_loop(0, 64, kinetic, 0)

    wait_recv(ag2, ag2_recv)

    def correct(p, _):
        pot, dr, di = (jnp.concatenate([ag2[p, q], ag2[8 + p, q]], axis=0) for q in range(3))
        row = pl.multiple_of((p + 3) * 8, 8)
        at = pl.ds(row, 8)

        def one(m, _):
            vol = m * 4
            ur, ui, vr, vi = (p_buf[vol + k, at, :] for k in range(4))
            gur, gui, gvr, gvi = (b_buf[vol + k, at, :] for k in range(4))
            to = pl.ds(p, 8, stride=8)
            o_ref[vol, to, :] = 0.5 * (gur + (pot * ui + dr * vi + di * vr))
            o_ref[vol + 1, to, :] = 0.5 * (gui - (pot * ur + dr * vr - di * vi))
            o_ref[vol + 2, to, :] = 0.5 * (gvr + (dr * ui - di * ur - pot * vi))
            o_ref[vol + 3, to, :] = 0.5 * (gvi - (dr * ur + di * ui - pot * vr))
            return 0

        lax.fori_loop(0, 8, one, 0)
        return 0

    lax.fori_loop(0, 8, correct, 0)

    wait_send(rs1_copy)
    wait_send(ag1_copy)
    wait_send(rs2_copy)
    wait_send(ag2_copy)
    halo_copy(0).wait_send()
    halo_copy(1).wait_send()

    def moves_sent(s, _):
        near_copy(s).wait_send()
        third_copy(s).wait_send()
        for c in range(2):
            far_copy(c, s).wait_send()
            forward_copy(c, s).wait_send()
        return 0

    lax.fori_loop(0, 4, moves_sent, 0)


def local(cloud_states, cloud_shift, boost_wave):
    f32 = jnp.float32
    angles = 2.0 * math.pi / NZ * np.arange(NZ)
    cos = jnp.asarray(np.cos(angles), f32)
    sin = jnp.asarray(np.sin(angles), f32)
    smem = pl.BlockSpec(memory_space=pltpu.SMEM)
    dma = pltpu.SemaphoreType.DMA
    out = pl.pallas_call(
        kernel,
        out_shape=jax.ShapeDtypeStruct((32, 64, 128), f32),
        in_specs=[smem, smem, smem, smem, pl.BlockSpec(memory_space=pl.ANY)],
        out_specs=pl.BlockSpec(memory_space=pltpu.VMEM),
        scratch_shapes=[
            pltpu.VMEM((4, 2, 4, 4, 8, 1024), f32),
            pltpu.VMEM((2, 4, 256, 128), f32),
            pltpu.VMEM((32, 112, 128), f32),
            pltpu.VMEM((32, 112, 128), f32),
            pltpu.VMEM((384, 128), f32),
            pltpu.VMEM((16, 24, 128), f32),
            pltpu.VMEM((24, 128), f32),
            pltpu.VMEM((2, 24, 128), f32),
            pltpu.VMEM((24, 128), f32),
            pltpu.VMEM((16, 24, 128), f32),
            pltpu.VMEM((192, 128), f32),
            pltpu.VMEM((192, 128), f32),
            pltpu.VMEM((16, 3, 4, 128), f32),
            pltpu.VMEM((16, 3, 4, 128), f32),
            pltpu.VMEM((3, 4, 128), f32),
            pltpu.VMEM((16, 3, 4, 128), f32),
            dma((2,)), dma((3, 2, 4)), dma((3, 2, 4)),
            dma((16,)), dma((16,)), dma((2,)), dma((2,)), dma((16,)), dma((16,)),
            dma((16,)), dma((16,)), dma((16,)), dma((16,)), dma((2,)), dma((2,)),
        ],
        compiler_params=pltpu.CompilerParams(
            collective_id=0, has_side_effects=True, vmem_limit_bytes=40 * 2**20),
    )(cloud_shift, boost_wave, cos, sin, cloud_states)
    out = out.reshape(2, 4, 4, 8, 8, 128).transpose(0, 1, 2, 4, 3, 5)
    return out.reshape(2, 4, 4, 8, 1024)


def solution(mesh):
    in_specs = (P(None, "grp", None, "slab", None), P(), P())
    out_specs = P(None, "grp", None, "slab", None)
    return jax.shard_map(local, mesh=mesh, in_specs=in_specs, out_specs=out_specs, check_vma=False)
```

```python
import math

import jax
import jax.numpy as jnp
from jax import lax
from jax.experimental import pallas as pl
from jax.experimental.pallas import tpu as pltpu
from jax.sharding import PartitionSpec as P

MESH = pl.DeviceIdType.MESH
W = (-49.0 / 18.0, 1.5, -0.15, 1.0 / 90.0)
DT = 0.1
VMEM_LIMIT = 60 * 2**20
NZ = 128
STATES = 64
M = 4
ONE, THREE, TWO = 0, 1, 2


def stencil_tables(scale):
    lane = lax.broadcasted_iota(jnp.int32, (8, 128), 1)
    sub = lax.broadcasted_iota(jnp.int32, (8, 128), 0)
    y = lane % 32
    w = [scale * v for v in W]
    cy = {}
    for s in (1, -1, 2, -2, 3, -3):
        cy[s] = jnp.where((y + s >= 0) & (y + s < 32), w[abs(s)], 0.0)
    m32 = jnp.where(lane >= 32, w[1], w[3])
    m96 = jnp.where(lane < 96, w[1], w[3])
    up = [jnp.where((lane < 32 * j) & (sub < 7), w[j], 0.0) for j in (1, 2, 3)]
    down = [jnp.where((lane >= 128 - 32 * j) & (sub > 0), w[j], 0.0) for j in (1, 2, 3)]
    return w, cy, m32, m96, up, down


def laplacian(tables, ref, vol, row):
    w, cy, m32, m96, up, down = tables

    def plane(d):
        return ref[vol, pl.ds(pl.multiple_of(row + 8 * d, 8), 8 * M), :].reshape(M, 8, 128)

    f = plane(0)
    t = (3.0 * w[0]) * f
    for j in (1, 2, 3):
        t = t + w[j] * (plane(-j) + plane(j))
    for s in (1, -1, 2, -2, 3, -3):
        t = t + cy[s] * pltpu.roll(f, (-s) % 128, 2)
    r32, r64, r96 = (pltpu.roll(f, 32 * j, 2) for j in (1, 2, 3))
    t = t + m32 * r32 + w[2] * r64 + m96 * r96
    above = up[0] * r32 + up[1] * r64 + up[2] * r96
    below = down[0] * r96 + down[1] * r64 + down[2] * r32
    return f, t + pltpu.roll(above, 1, 1) + pltpu.roll(below, 7, 1)


def two_thirds(n):
    y = jnp.exp(jnp.log(jnp.maximum(n, 1e-30)) * (1.0 / 3.0))
    y = y - (y * y * y - n) / (3.0 * y * y)
    return y * y


def kernel(shift_ref, boost_ref, x_ref, o_ref,
           x_buf, land, e_buf, b_buf, p_buf, trig, d1, rs1, t1, s1, sel1, ag1, f0, acc, d2, rs2, t2, ag2,
           x_sem, slab_send, slab_recv, rs1_send, rs1_recv, s1_send, s1_recv, ag1_send, ag1_recv,
           rs2_send, rs2_recv, ag2_send, ag2_recv, halo_send, halo_recv):
    slabs = lax.axis_size("slab")
    groups = lax.axis_size("grp")
    i = lax.axis_index("slab")
    g = lax.axis_index("grp")
    core = lax.rem(i, 2)
    mate = i + 1 - 2 * core

    def slab(d):
        return (lax.rem(i + d + slabs, slabs), g)

    def peer(k):
        return (i, lax.rem(g + k, groups))

    def own_copy(c):
        return pltpu.make_async_copy(x_ref.at[c], x_buf.at[c], x_sem.at[c])

    own_copy(0).start()
    own_copy(1).start()

    barrier = pltpu.get_barrier_semaphore()
    for d in (1, -1, 2, -2, 3, -3):
        pl.semaphore_signal(barrier, inc=1, device_id=slab(d), device_id_type=MESH)

    def greet(k, _):
        pl.semaphore_signal(barrier, inc=1, device_id=peer(k), device_id_type=MESH)
        return 0

    lax.fori_loop(1, groups, greet, 0)

    for c in range(2):
        own_copy(c).wait()

        def relay(m, _):
            s = m // 4
            k = lax.rem(m, 4)
            for j in range(8):
                land[c, s, k, pl.ds(192 - 192 * c + j, 8, stride=8), :] = x_buf[c, s, k, :, 128 * j:128 * j + 128]
            return 0

        lax.fori_loop(0, 16, relay, 0)

        def terms(p, _):
            at = pl.ds(pl.multiple_of(192 - 192 * c + 8 * p, 8), 8)
            n = kr = ki = None
            for s in range(4):
                ur, ui, vr, vi = (land[c, s, k, at, :] for k in range(4))
                a = vr * vr + vi * vi
                b = ur * vr + ui * vi
                e = ui * vr - ur * vi
                n, kr, ki = (a, b, e) if s == 0 else (n + a, kr + b, ki + e)
            for q, v in enumerate((n, kr, ki)):
                d1[c * 8 + p, q] = v
            return 0

        lax.fori_loop(0, 8, terms, 0)

    def phases(m, _):
        c = m // 14
        q = lax.rem(m, 14)
        index = (boost_ref[c] * (8 * i + q - 3)) & (NZ - 1)
        angle = jnp.full((8, 128), index, jnp.int32).astype(jnp.float32) * (2.0 * math.pi / NZ)
        trig[c, q, 0] = jnp.cos(angle)
        trig[c, q, 1] = jnp.sin(angle)
        return 0

    lax.fori_loop(0, 28, phases, 0)
    acc[...] = jnp.zeros_like(acc)

    pl.semaphore_wait(barrier, 6 + groups - 1)

    def start(make):
        def body(k, _):
            make(k).start()
            return 0
        lax.fori_loop(1, groups, body, 0)

    def wait_send(make):
        def body(k, _):
            make(k).wait_send()
            return 0
        lax.fori_loop(1, groups, body, 0)

    def wait_recv(buf, sem):
        def body(k, _):
            o = lax.rem(g + k, groups)
            pltpu.make_async_copy(buf.at[o], buf.at[o], sem.at[o]).wait()
            return 0
        lax.fori_loop(1, groups, body, 0)

    def scatter(src, dst, send, recv):
        def make(k):
            o = lax.rem(g + k, groups)
            return pltpu.make_async_remote_copy(
                src_ref=src.at[o], dst_ref=dst.at[g], send_sem=send.at[o], recv_sem=recv.at[g],
                device_id=peer(k), device_id_type=MESH)
        return make

    def gather(src, dst, send, recv):
        def make(k):
            o = lax.rem(g + k, groups)
            return pltpu.make_async_remote_copy(
                src_ref=src, dst_ref=dst.at[g], send_sem=send.at[o], recv_sem=recv.at[g],
                device_id=peer(k), device_id_type=MESH)
        return make

    rs1_copy = scatter(d1, rs1, rs1_send, rs1_recv)
    ag1_copy = gather(sel1, ag1, ag1_send, ag1_recv)
    rs2_copy = scatter(d2, rs2, rs2_send, rs2_recv)
    ag2_copy = gather(t2, ag2, ag2_send, ag2_recv)

    def window(c, s, first, planes):
        return land.at[c, s, :, pl.ds(pl.multiple_of(first * 8, 8), planes * 8)]

    def move(slot, c, s, src, dst, planes, device):
        return pltpu.make_async_remote_copy(
            src_ref=window(c, s, src, planes), dst_ref=window(c, s, dst, planes),
            send_sem=slab_send.at[slot, c, s], recv_sem=slab_recv.at[slot, c, s],
            device_id=device, device_id_type=MESH)

    def far_copy(c, s):
        return move(TWO, c, s, 24 - 24 * c, 8 + 8 * c, 8, slab(2 - 4 * c))

    def near_copy(s):
        return move(ONE, core, s, 24 - 24 * core, 16 - 8 * core, 8, (mate, g))

    def third_copy(s):
        return move(THREE, 1 - core, s, 30 * core, 24 - 18 * core, 2, slab(6 * core - 3))

    def forward_one(s):
        return move(ONE, 1 - core, s, 16 - 8 * core, 8 + 8 * core, 8, (mate, g))

    def forward_three(s):
        return move(THREE, core, s, 14 + 2 * core, 6 + 18 * core, 2, (mate, g))

    def arrived(slot, c, s, planes):
        here = window(c, s, 0, planes)
        pltpu.make_async_copy(here, here, slab_recv.at[slot, c, s]).wait()

    def start_moves(s, _):
        far_copy(0, s).start()
        far_copy(1, s).start()
        near_copy(s).start()
        third_copy(s).start()
        return 0

    def forward(s):
        arrived(TWO, 0, s, 8)
        arrived(TWO, 1, s, 8)
        forward_one(s).start()
        forward_three(s).start()

    start(rs1_copy)
    lax.fori_loop(0, 4, start_moves, 0)
    rs1[g] = d1[g]

    wait_recv(rs1, rs1_recv)

    def add1(k, total):
        return total + rs1[k]

    t1[...] = lax.fori_loop(1, groups, add1, rs1[0])
    cloud = g // 8
    plane_own = lax.rem(g, 8)
    way = 1 - 2 * cloud

    def s1_copy(d):
        return pltpu.make_async_remote_copy(
            src_ref=t1, dst_ref=s1.at[d - 1], send_sem=s1_send.at[d - 1], recv_sem=s1_recv.at[d - 1],
            device_id=slab(way * d), device_id_type=MESH)

    s1_copy(1).start()
    s1_copy(2).start()
    forward(0)
    s1_copy(1).wait_recv()
    s1_copy(2).wait_recv()
    r0 = shift_ref[0] - 8
    r1 = shift_ref[1] - 8
    steps = plane_own * way + 7 * cloud + shift_ref[cloud] - 8
    sel1[...] = s1[(steps >> 3) & 1]
    start(ag1_copy)
    ag1[g] = sel1[...]
    forward(1)
    wait_recv(ag1, ag1_recv)

    def fields_now(p, _):
        n = kr = ki = None
        for c in range(2):
            src = 8 * c + ((p - r0 if c == 0 else p + r1) & 7)
            cos, sin = trig[c, p + 3, 0], trig[c, p + 3, 1]
            cos, sin = cos * cos - sin * sin, 2.0 * cos * sin
            a, b, e = ag1[src, 0], ag1[src, 1], ag1[src, 2]
            b, e = b * cos - e * sin, b * sin + e * cos
            n, kr, ki = (a, b, e) if c == 0 else (n + a, kr + b, ki + e)
        f0[0, p] = DT * (1.2 * two_thirds(n * (1.0 / STATES)) - 1.0)
        f0[1, p] = kr * (-3.0 * DT / STATES)
        f0[2, p] = ki * (-3.0 * DT / STATES)
        return 0

    lax.fori_loop(0, 8, fields_now, 0)

    tables = stencil_tables(0.5 * DT)

    def halo_copy(d, s):
        src = pl.ds(24, 24) if d == 0 else pl.ds(64, 24)
        dst = pl.ds(88, 24) if d == 0 else pl.ds(0, 24)
        vols = pl.ds(s * 8, 8)
        return pltpu.make_async_remote_copy(
            src_ref=p_buf.at[vols, src], dst_ref=p_buf.at[vols, dst],
            send_sem=halo_send.at[d, s], recv_sem=halo_recv.at[d, s],
            device_id=slab(2 * d - 1), device_id_type=MESH)

    def send_halos(s):
        halo_copy(0, s).start()
        halo_copy(1, s).start()

    def state_step(s, _):
        for c in range(2):
            arrived(ONE, c, s, 8)
            arrived(THREE, c, s, 2)
            for k in range(4):
                e_buf[k] = land[c, s, k, 48:208, :].reshape(20, 8, 128)
            vol = (s * 2 + c) * 4
            base = 7 - r0 if c == 0 else r1 - 1

            def boost(q, _):
                cos, sin = trig[c, q, 0], trig[c, q, 1]
                plane = jnp.maximum(jnp.minimum(base + q, 19), 0)
                ur, ui, vr, vi = (e_buf[k, plane] for k in range(4))
                to = pl.ds(pl.multiple_of(q * 8, 8), 8)
                b_buf[vol, to, :] = ur * cos - ui * sin
                b_buf[vol + 1, to, :] = ur * sin + ui * cos
                b_buf[vol + 2, to, :] = vr * cos + vi * sin
                b_buf[vol + 3, to, :] = vi * cos - vr * sin
                return 0

            lax.fori_loop(0, 14, boost, 0)

            def predict(m, _):
                p = m * M
                row = pl.multiple_of((p + 3) * 8, 8)
                pot, dr, di = (f0[q, pl.ds(p, M)] for q in range(3))
                ur, lur = laplacian(tables, b_buf, vol, row)
                ui, lui = laplacian(tables, b_buf, vol + 1, row)
                vr, lvr = laplacian(tables, b_buf, vol + 2, row)
                vi, lvi = laplacian(tables, b_buf, vol + 3, row)
                pur = ur - lui + (pot * ui + dr * vi + di * vr)
                pui = ui + lur - (pot * ur + dr * vr - di * vi)
                pvr = vr + lvi + (dr * ui - di * ur - pot * vi)
                pvi = vi - lvr - (dr * ur + di * ui - pot * vr)
                at = pl.ds(row, 8 * M)
                for k, v in enumerate((pur, pui, pvr, pvi)):
                    p_buf[vol + k, at, :] = v.reshape(8 * M, 128)
                acc[0, pl.ds(p, M)] += pvr * pvr + pvi * pvi
                acc[1, pl.ds(p, M)] += pur * pvr + pui * pvi
                acc[2, pl.ds(p, M)] += pui * pvr - pur * pvi
                return 0

            lax.fori_loop(0, 8 // M, predict, 0)

        @pl.when(s < 2)
        def _():
            forward(s + 2)

        @pl.when(s == 1)
        def _():
            send_halos(0)
            send_halos(1)

        @pl.when(s == 2)
        def _():
            send_halos(2)

        return 0

    lax.fori_loop(0, 4, state_step, 0)

    for p in range(8):
        for q in range(3):
            v = acc[q, p]
            d2[p, q] = v[0:4]
            d2[8 + p, q] = v[4:8]

    start(rs2_copy)
    send_halos(3)
    rs2[g] = d2[g]
    wait_recv(rs2, rs2_recv)

    def add2(k, total):
        return total + rs2[k]

    n, kr, ki = lax.fori_loop(1, groups, add2, rs2[0])
    t2[0] = DT * (1.2 * two_thirds(n * (1.0 / STATES)) - 1.0)
    t2[1] = kr * (-3.0 * DT / STATES)
    t2[2] = ki * (-3.0 * DT / STATES)
    start(ag2_copy)
    ag2[g] = t2[...]

    def kinetic_state(s, _):
        halo_copy(0, s).wait_recv()
        halo_copy(1, s).wait_recv()

        def kinetic(m, _):
            vol = (s * 2 + m // (8 // M)) * 4
            row = pl.multiple_of((lax.rem(m, 8 // M) * M + 3) * 8, 8)
            at = pl.ds(row, 8 * M)
            ur, lur = laplacian(tables, p_buf, vol, row)
            ui, lui = laplacian(tables, p_buf, vol + 1, row)
            vr, lvr = laplacian(tables, p_buf, vol + 2, row)
            vi, lvi = laplacian(tables, p_buf, vol + 3, row)
            for k, v in enumerate((ur - lui, ui + lur, vr + lvi, vi - lvr)):
                b_buf[vol + k, at, :] += v.reshape(8 * M, 128)
            return 0

        lax.fori_loop(0, 16 // M, kinetic, 0)
        return 0

    lax.fori_loop(0, 4, kinetic_state, 0)
    wait_recv(ag2, ag2_recv)

    def correct(p, _):
        pot, dr, di = (jnp.concatenate([ag2[p, q], ag2[8 + p, q]], axis=0) for q in range(3))
        at = pl.ds(pl.multiple_of((p + 3) * 8, 8), 8)
        to = pl.ds(p, 8, stride=8)
        for s in range(4):
            for c in range(2):
                vol = (s * 2 + c) * 4
                out = (c * 4 + s) * 4
                ur, ui, vr, vi = (p_buf[vol + k, at, :] for k in range(4))
                gur, gui, gvr, gvi = (b_buf[vol + k, at, :] for k in range(4))
                o_ref[out, to, :] = 0.5 * (gur + (pot * ui + dr * vi + di * vr))
                o_ref[out + 1, to, :] = 0.5 * (gui - (pot * ur + dr * vr - di * vi))
                o_ref[out + 2, to, :] = 0.5 * (gvr + (dr * ui - di * ur - pot * vi))
                o_ref[out + 3, to, :] = 0.5 * (gvi - (dr * ur + di * ui - pot * vr))
        return 0

    lax.fori_loop(0, 8, correct, 0)

    for make in (rs1_copy, ag1_copy, rs2_copy, ag2_copy):
        wait_send(make)
    s1_copy(1).wait_send()
    s1_copy(2).wait_send()

    def moves_sent(s, _):
        for c in range(2):
            far_copy(c, s).wait_send()
            halo_copy(c, s).wait_send()
        near_copy(s).wait_send()
        third_copy(s).wait_send()
        forward_one(s).wait_send()
        forward_three(s).wait_send()
        return 0

    lax.fori_loop(0, 4, moves_sent, 0)


def local(cloud_states, cloud_shift, boost_wave):
    f32 = jnp.float32
    smem = pl.BlockSpec(memory_space=pltpu.SMEM)
    dma = pltpu.SemaphoreType.DMA
    out = pl.pallas_call(
        kernel,
        out_shape=jax.ShapeDtypeStruct((32, 64, 128), f32),
        in_specs=[smem, smem, pl.BlockSpec(memory_space=pl.ANY)],
        out_specs=pl.BlockSpec(memory_space=pltpu.VMEM),
        scratch_shapes=[
            pltpu.VMEM((2, 4, 4, 8, 1024), f32),
            pltpu.VMEM((2, 4, 4, 256, 128), f32),
            pltpu.VMEM((4, 20, 8, 128), f32),
            pltpu.VMEM((32, 112, 128), f32),
            pltpu.VMEM((32, 112, 128), f32),
            pltpu.VMEM((2, 14, 2, 8, 128), f32),
            pltpu.VMEM((16, 3, 8, 128), f32),
            pltpu.VMEM((16, 3, 8, 128), f32),
            pltpu.VMEM((3, 8, 128), f32),
            pltpu.VMEM((2, 3, 8, 128), f32),
            pltpu.VMEM((3, 8, 128), f32),
            pltpu.VMEM((16, 3, 8, 128), f32),
            pltpu.VMEM((3, 8, 8, 128), f32),
            pltpu.VMEM((3, 8, 8, 128), f32),
            pltpu.VMEM((16, 3, 4, 128), f32),
            pltpu.VMEM((16, 3, 4, 128), f32),
            pltpu.VMEM((3, 4, 128), f32),
            pltpu.VMEM((16, 3, 4, 128), f32),
            dma((2,)), dma((3, 2, 4)), dma((3, 2, 4)),
            dma((16,)), dma((16,)), dma((2,)), dma((2,)), dma((16,)), dma((16,)),
            dma((16,)), dma((16,)), dma((16,)), dma((16,)), dma((2, 4)), dma((2, 4)),
        ],
        compiler_params=pltpu.CompilerParams(
            collective_id=0, has_side_effects=True, vmem_limit_bytes=VMEM_LIMIT),
    )(cloud_shift, boost_wave, cloud_states)
    out = out.reshape(2, 4, 4, 8, 8, 128).transpose(0, 1, 2, 4, 3, 5)
    return out.reshape(2, 4, 4, 8, 1024)


def solution(mesh):
    in_specs = (P(None, "grp", None, "slab", None), P(), P())
    out_specs = P(None, "grp", None, "slab", None)
    return jax.shard_map(local, mesh=mesh, in_specs=in_specs, out_specs=out_specs, check_vma=False)
```

```python
import math

import jax
import jax.numpy as jnp
from jax import lax
from jax.experimental import pallas as pl
from jax.experimental.pallas import tpu as pltpu
from jax.sharding import PartitionSpec as P

MESH = pl.DeviceIdType.MESH
W = (-49.0 / 18.0, 1.5, -0.15, 1.0 / 90.0)
DT = 0.1
VMEM_LIMIT = 44 * 2**20
NZ = 128
STATES = 64
M = 4
ONE, THREE, TWO = 0, 1, 2


def stencil_tables(scale):
    lane = lax.broadcasted_iota(jnp.int32, (8, 128), 1)
    sub = lax.broadcasted_iota(jnp.int32, (8, 128), 0)
    y = lane % 32
    w = [scale * v for v in W]
    cy = {}
    for s in (1, -1, 2, -2, 3, -3):
        cy[s] = jnp.where((y + s >= 0) & (y + s < 32), w[abs(s)], 0.0)
    m32 = jnp.where(lane >= 32, w[1], w[3])
    m96 = jnp.where(lane < 96, w[1], w[3])
    up = [jnp.where((lane < 32 * j) & (sub < 7), w[j], 0.0) for j in (1, 2, 3)]
    down = [jnp.where((lane >= 128 - 32 * j) & (sub > 0), w[j], 0.0) for j in (1, 2, 3)]
    return w, cy, m32, m96, up, down


def laplacian(tables, ref, vol, row):
    w, cy, m32, m96, up, down = tables

    def plane(d):
        return ref[vol, pl.ds(pl.multiple_of(row + 8 * d, 8), 8 * M), :].reshape(M, 8, 128)

    f = plane(0)
    t = (3.0 * w[0]) * f
    for j in (1, 2, 3):
        t = t + w[j] * (plane(-j) + plane(j))
    for s in (1, -1, 2, -2, 3, -3):
        t = t + cy[s] * pltpu.roll(f, (-s) % 128, 2)
    r32, r64, r96 = (pltpu.roll(f, 32 * j, 2) for j in (1, 2, 3))
    t = t + m32 * r32 + w[2] * r64 + m96 * r96
    above = up[0] * r32 + up[1] * r64 + up[2] * r96
    below = down[0] * r96 + down[1] * r64 + down[2] * r32
    return f, t + pltpu.roll(above, 1, 1) + pltpu.roll(below, 7, 1)


def two_thirds(n):
    y = jnp.exp(jnp.log(jnp.maximum(n, 1e-30)) * (1.0 / 3.0))
    y = y - (y * y * y - n) / (3.0 * y * y)
    return y * y


def kernel(shift_ref, boost_ref, x_ref, o_ref,
           x_buf, land, e_buf, b_buf, p_buf, trig, d1, rs1, t1, s1, sel1, ag1, f0, acc, d2, rs2, t2, ag2,
           x_sem, slab_send, slab_recv, rs1_send, rs1_recv, s1_send, s1_recv, ag1_send, ag1_recv,
           rs2_send, rs2_recv, ag2_send, ag2_recv, halo_send, halo_recv):
    slabs = lax.axis_size("slab")
    groups = lax.axis_size("grp")
    i = lax.axis_index("slab")
    g = lax.axis_index("grp")
    core = lax.rem(i, 2)
    mate = i + 1 - 2 * core

    def slab(d):
        return (lax.rem(i + d + slabs, slabs), g)

    def peer(k):
        return (i, lax.rem(g + k, groups))

    def own_copy(c):
        return pltpu.make_async_copy(x_ref.at[c], x_buf.at[c], x_sem.at[c])

    own_copy(0).start()
    own_copy(1).start()

    barrier = pltpu.get_barrier_semaphore()
    for d in (1, -1, 2, -2, 3, -3):
        pl.semaphore_signal(barrier, inc=1, device_id=slab(d), device_id_type=MESH)
    for d in (1, -1, 2, -2):
        pl.semaphore_signal(barrier, inc=1, device_id=(slab(d)[0], lax.rem(g + 8, groups)), device_id_type=MESH)

    def greet(k, _):
        pl.semaphore_signal(barrier, inc=1, device_id=peer(k), device_id_type=MESH)
        return 0

    lax.fori_loop(1, groups, greet, 0)

    for c in range(2):
        own_copy(c).wait()

        def relay(m, _):
            s = m // 4
            k = lax.rem(m, 4)
            for j in range(8):
                land[c, s, k, pl.ds(192 - 192 * c + j, 8, stride=8), :] = x_buf[c, s, k, :, 128 * j:128 * j + 128]
            return 0

        lax.fori_loop(0, 16, relay, 0)

        def terms(p, _):
            at = pl.ds(pl.multiple_of(192 - 192 * c + 8 * p, 8), 8)
            n = kr = ki = None
            for s in range(4):
                ur, ui, vr, vi = (land[c, s, k, at, :] for k in range(4))
                a = vr * vr + vi * vi
                b = ur * vr + ui * vi
                e = ui * vr - ur * vi
                n, kr, ki = (a, b, e) if s == 0 else (n + a, kr + b, ki + e)
            for q, v in enumerate((n, kr, ki)):
                d1[p, c, q] = v
            return 0

        lax.fori_loop(0, 8, terms, 0)

    def phases(m, _):
        c = m // 14
        q = lax.rem(m, 14)
        index = (boost_ref[c] * (8 * i + q - 3)) & (NZ - 1)
        angle = jnp.full((8, 128), index, jnp.int32).astype(jnp.float32) * (2.0 * math.pi / NZ)
        trig[c, q, 0] = jnp.cos(angle)
        trig[c, q, 1] = jnp.sin(angle)
        return 0

    lax.fori_loop(0, 28, phases, 0)
    acc[...] = jnp.zeros_like(acc)

    pl.semaphore_wait(barrier, 10 + groups - 1)

    column = g // 8
    z_own = lax.rem(g, 8)

    def in_group(k):
        return lax.rem(g + k, groups)

    def in_column(k):
        return column * 8 + lax.rem(z_own + k, 8)

    def start(make, count):
        def body(k, _):
            make(k).start()
            return 0
        lax.fori_loop(1, count, body, 0)

    def wait_send(make, count):
        def body(k, _):
            make(k).wait_send()
            return 0
        lax.fori_loop(1, count, body, 0)

    def wait_recv(buf, sem, count, mine):
        def body(k, _):
            o = lax.rem(mine + k, count)
            pltpu.make_async_copy(buf.at[o], buf.at[o], sem.at[o]).wait()
            return 0
        lax.fori_loop(1, count, body, 0)

    def exchange(src, dst, send, recv, one, count, mine):
        def make(k):
            o = lax.rem(mine + k, count)
            to = in_group(k) if count == groups else in_column(k)
            return pltpu.make_async_remote_copy(
                src_ref=src if one else src.at[o], dst_ref=dst.at[mine], send_sem=send.at[o], recv_sem=recv.at[mine],
                device_id=(i, to), device_id_type=MESH)
        return make

    rs1_copy = exchange(d1, rs1, rs1_send, rs1_recv, False, 8, z_own)
    ag1_copy = exchange(sel1, ag1, ag1_send, ag1_recv, True, 8, z_own)
    rs2_copy = exchange(d2, rs2, rs2_send, rs2_recv, False, groups, g)
    ag2_copy = exchange(t2, ag2, ag2_send, ag2_recv, True, groups, g)

    def window(c, s, first, planes):
        return land.at[c, s, :, pl.ds(pl.multiple_of(first * 8, 8), planes * 8)]

    def move(slot, c, s, src, dst, planes, device):
        return pltpu.make_async_remote_copy(
            src_ref=window(c, s, src, planes), dst_ref=window(c, s, dst, planes),
            send_sem=slab_send.at[slot, c, s], recv_sem=slab_recv.at[slot, c, s],
            device_id=device, device_id_type=MESH)

    def far_copy(c, s):
        return move(TWO, c, s, 24 - 24 * c, 8 + 8 * c, 8, slab(2 - 4 * c))

    def near_copy(s):
        return move(ONE, core, s, 24 - 24 * core, 16 - 8 * core, 8, (mate, g))

    def third_copy(s):
        return move(THREE, 1 - core, s, 30 * core, 24 - 18 * core, 2, slab(6 * core - 3))

    def forward_one(s):
        return move(ONE, 1 - core, s, 16 - 8 * core, 8 + 8 * core, 8, (mate, g))

    def forward_three(s):
        return move(THREE, core, s, 14 + 2 * core, 6 + 18 * core, 2, (mate, g))

    def arrived(slot, c, s, planes):
        here = window(c, s, 0, planes)
        pltpu.make_async_copy(here, here, slab_recv.at[slot, c, s]).wait()

    def start_moves(s, _):
        far_copy(0, s).start()
        far_copy(1, s).start()
        near_copy(s).start()
        third_copy(s).start()
        return 0

    def forward(s):
        arrived(TWO, 0, s, 8)
        arrived(TWO, 1, s, 8)
        forward_one(s).start()
        forward_three(s).start()

    start(rs1_copy, 8)
    lax.fori_loop(0, 4, start_moves, 0)
    rs1[z_own] = d1[z_own]

    wait_recv(rs1, rs1_recv, 8, z_own)

    def add1(k, total):
        return total + rs1[k]

    t1[...] = lax.fori_loop(1, 8, add1, rs1[0])

    def s1_copy(c, d, x):
        return pltpu.make_async_remote_copy(
            src_ref=t1.at[c], dst_ref=s1.at[c, d, column], send_sem=s1_send.at[c, d, x], recv_sem=s1_recv.at[c, d, column],
            device_id=(slab((1 - 2 * c) * (d + 1))[0], x * 8 + z_own), device_id_type=MESH)

    cases = [(c, d, x) for c in range(2) for d in range(2) for x in range(2)]
    for case in cases:
        s1_copy(*case).start()
    forward(0)
    for c, d, x in cases:
        pltpu.make_async_copy(s1.at[c, d, x], s1.at[c, d, x], s1_recv.at[c, d, x]).wait()
    r0 = shift_ref[0] - 8
    r1 = shift_ref[1] - 8
    from_0 = ((z_own + r0) >> 3) & 1
    from_1 = ((7 - z_own + r1) >> 3) & 1
    sel1[0] = s1[0, from_0, 0] + s1[0, from_0, 1]
    sel1[1] = s1[1, from_1, 0] + s1[1, from_1, 1]
    start(ag1_copy, 8)
    ag1[z_own] = sel1[...]
    forward(1)
    wait_recv(ag1, ag1_recv, 8, z_own)

    def fields_now(p, _):
        n = kr = ki = None
        for c in range(2):
            src = (p - r0 if c == 0 else p + r1) & 7
            cos, sin = trig[c, p + 3, 0], trig[c, p + 3, 1]
            cos, sin = cos * cos - sin * sin, 2.0 * cos * sin
            a, b, e = ag1[src, c, 0], ag1[src, c, 1], ag1[src, c, 2]
            b, e = b * cos - e * sin, b * sin + e * cos
            n, kr, ki = (a, b, e) if c == 0 else (n + a, kr + b, ki + e)
        f0[0, p] = DT * (1.2 * two_thirds(n * (1.0 / STATES)) - 1.0)
        f0[1, p] = kr * (-3.0 * DT / STATES)
        f0[2, p] = ki * (-3.0 * DT / STATES)
        return 0

    lax.fori_loop(0, 8, fields_now, 0)

    tables = stencil_tables(0.5 * DT)

    def halo_copy(d, s):
        src = pl.ds(24, 24) if d == 0 else pl.ds(64, 24)
        dst = pl.ds(88, 24) if d == 0 else pl.ds(0, 24)
        vols = pl.ds(s * 8, 8)
        return pltpu.make_async_remote_copy(
            src_ref=p_buf.at[vols, src], dst_ref=p_buf.at[vols, dst],
            send_sem=halo_send.at[d, s], recv_sem=halo_recv.at[d, s],
            device_id=slab(2 * d - 1), device_id_type=MESH)

    def send_halos(s):
        halo_copy(0, s).start()
        halo_copy(1, s).start()

    def state_step(s, _):
        for c in range(2):
            arrived(ONE, c, s, 8)
            arrived(THREE, c, s, 2)
            for k in range(4):
                e_buf[k] = land[c, s, k, 48:208, :].reshape(20, 8, 128)
            vol = (s * 2 + c) * 4
            base = 7 - r0 if c == 0 else r1 - 1

            def boost(q, _):
                cos, sin = trig[c, q, 0], trig[c, q, 1]
                plane = jnp.maximum(jnp.minimum(base + q, 19), 0)
                ur, ui, vr, vi = (e_buf[k, plane] for k in range(4))
                to = pl.ds(pl.multiple_of(q * 8, 8), 8)
                b_buf[vol, to, :] = ur * cos - ui * sin
                b_buf[vol + 1, to, :] = ur * sin + ui * cos
                b_buf[vol + 2, to, :] = vr * cos + vi * sin
                b_buf[vol + 3, to, :] = vi * cos - vr * sin
                return 0

            lax.fori_loop(0, 14, boost, 0)

            def predict(m, _):
                p = m * M
                row = pl.multiple_of((p + 3) * 8, 8)
                pot, dr, di = (f0[q, pl.ds(p, M)] for q in range(3))
                ur, lur = laplacian(tables, b_buf, vol, row)
                ui, lui = laplacian(tables, b_buf, vol + 1, row)
                vr, lvr = laplacian(tables, b_buf, vol + 2, row)
                vi, lvi = laplacian(tables, b_buf, vol + 3, row)
                pur = ur - lui + (pot * ui + dr * vi + di * vr)
                pui = ui + lur - (pot * ur + dr * vr - di * vi)
                pvr = vr + lvi + (dr * ui - di * ur - pot * vi)
                pvi = vi - lvr - (dr * ur + di * ui - pot * vr)
                at = pl.ds(row, 8 * M)
                for k, v in enumerate((pur, pui, pvr, pvi)):
                    p_buf[vol + k, at, :] = v.reshape(8 * M, 128)
                acc[0, pl.ds(p, M)] += pvr * pvr + pvi * pvi
                acc[1, pl.ds(p, M)] += pur * pvr + pui * pvi
                acc[2, pl.ds(p, M)] += pui * pvr - pur * pvi
                return 0

            lax.fori_loop(0, 8 // M, predict, 0)

        @pl.when(s < 2)
        def _():
            forward(s + 2)

        @pl.when(s == 1)
        def _():
            send_halos(0)
            send_halos(1)

        @pl.when(s == 2)
        def _():
            send_halos(2)

        return 0

    lax.fori_loop(0, 4, state_step, 0)

    for p in range(8):
        for q in range(3):
            v = acc[q, p]
            d2[p, q] = v[0:4]
            d2[8 + p, q] = v[4:8]

    start(rs2_copy, groups)
    send_halos(3)
    rs2[g] = d2[g]
    wait_recv(rs2, rs2_recv, groups, g)

    def add2(k, total):
        return total + rs2[k]

    n, kr, ki = lax.fori_loop(1, groups, add2, rs2[0])
    t2[0] = DT * (1.2 * two_thirds(n * (1.0 / STATES)) - 1.0)
    t2[1] = kr * (-3.0 * DT / STATES)
    t2[2] = ki * (-3.0 * DT / STATES)
    start(ag2_copy, groups)
    ag2[g] = t2[...]

    def kinetic_state(s, _):
        halo_copy(0, s).wait_recv()
        halo_copy(1, s).wait_recv()

        def kinetic(m, _):
            vol = (s * 2 + m // (8 // M)) * 4
            row = pl.multiple_of((lax.rem(m, 8 // M) * M + 3) * 8, 8)
            at = pl.ds(row, 8 * M)
            ur, lur = laplacian(tables, p_buf, vol, row)
            ui, lui = laplacian(tables, p_buf, vol + 1, row)
            vr, lvr = laplacian(tables, p_buf, vol + 2, row)
            vi, lvi = laplacian(tables, p_buf, vol + 3, row)
            for k, v in enumerate((ur - lui, ui + lur, vr + lvi, vi - lvr)):
                b_buf[vol + k, at, :] += v.reshape(8 * M, 128)
            return 0

        lax.fori_loop(0, 16 // M, kinetic, 0)
        return 0

    lax.fori_loop(0, 4, kinetic_state, 0)
    wait_recv(ag2, ag2_recv, groups, g)

    def correct(p, _):
        pot, dr, di = (jnp.concatenate([ag2[p, q], ag2[8 + p, q]], axis=0) for q in range(3))
        at = pl.ds(pl.multiple_of((p + 3) * 8, 8), 8)
        to = pl.ds(p, 8, stride=8)
        for s in range(4):
            for c in range(2):
                vol = (s * 2 + c) * 4
                out = (c * 4 + s) * 4
                ur, ui, vr, vi = (p_buf[vol + k, at, :] for k in range(4))
                gur, gui, gvr, gvi = (b_buf[vol + k, at, :] for k in range(4))
                o_ref[out, to, :] = 0.5 * (gur + (pot * ui + dr * vi + di * vr))
                o_ref[out + 1, to, :] = 0.5 * (gui - (pot * ur + dr * vr - di * vi))
                o_ref[out + 2, to, :] = 0.5 * (gvr + (dr * ui - di * ur - pot * vi))
                o_ref[out + 3, to, :] = 0.5 * (gvi - (dr * ur + di * ui - pot * vr))
        return 0

    lax.fori_loop(0, 8, correct, 0)

    wait_send(rs1_copy, 8)
    wait_send(ag1_copy, 8)
    wait_send(rs2_copy, groups)
    wait_send(ag2_copy, groups)
    for case in cases:
        s1_copy(*case).wait_send()

    def moves_sent(s, _):
        for c in range(2):
            far_copy(c, s).wait_send()
            halo_copy(c, s).wait_send()
        near_copy(s).wait_send()
        third_copy(s).wait_send()
        forward_one(s).wait_send()
        forward_three(s).wait_send()
        return 0

    lax.fori_loop(0, 4, moves_sent, 0)


def local(cloud_states, cloud_shift, boost_wave):
    f32 = jnp.float32
    smem = pl.BlockSpec(memory_space=pltpu.SMEM)
    dma = pltpu.SemaphoreType.DMA
    out = pl.pallas_call(
        kernel,
        out_shape=jax.ShapeDtypeStruct((32, 64, 128), f32),
        in_specs=[smem, smem, pl.BlockSpec(memory_space=pltpu.HBM)],
        out_specs=pl.BlockSpec(memory_space=pltpu.VMEM),
        scratch_shapes=[
            pltpu.VMEM((2, 4, 4, 8, 1024), f32),
            pltpu.VMEM((2, 4, 4, 256, 128), f32),
            pltpu.VMEM((4, 20, 8, 128), f32),
            pltpu.VMEM((32, 112, 128), f32),
            pltpu.VMEM((32, 112, 128), f32),
            pltpu.VMEM((2, 14, 2, 8, 128), f32),
            pltpu.VMEM((8, 2, 3, 8, 128), f32),
            pltpu.VMEM((8, 2, 3, 8, 128), f32),
            pltpu.VMEM((2, 3, 8, 128), f32),
            pltpu.VMEM((2, 2, 2, 3, 8, 128), f32),
            pltpu.VMEM((2, 3, 8, 128), f32),
            pltpu.VMEM((8, 2, 3, 8, 128), f32),
            pltpu.VMEM((3, 8, 8, 128), f32),
            pltpu.VMEM((3, 8, 8, 128), f32),
            pltpu.VMEM((16, 3, 4, 128), f32),
            pltpu.VMEM((16, 3, 4, 128), f32),
            pltpu.VMEM((3, 4, 128), f32),
            pltpu.VMEM((16, 3, 4, 128), f32),
            dma((2,)), dma((3, 2, 4)), dma((3, 2, 4)),
            dma((8,)), dma((8,)), dma((2, 2, 2)), dma((2, 2, 2)), dma((8,)), dma((8,)),
            dma((16,)), dma((16,)), dma((16,)), dma((16,)), dma((2, 4)), dma((2, 4)),
        ],
        compiler_params=pltpu.CompilerParams(
            collective_id=0, has_side_effects=True, vmem_limit_bytes=VMEM_LIMIT),
    )(cloud_shift, boost_wave, cloud_states)
    out = out.reshape(2, 4, 4, 8, 8, 128).transpose(0, 1, 2, 4, 3, 5)
    return out.reshape(2, 4, 4, 8, 1024)


def solution(mesh):
    in_specs = (P(None, "grp", None, "slab", None), P(), P())
    out_specs = P(None, "grp", None, "slab", None)
    return jax.shard_map(local, mesh=mesh, in_specs=in_specs, out_specs=out_specs, check_vma=False)
```

```python
import math

import jax
import jax.numpy as jnp
from jax import lax
from jax.experimental import pallas as pl
from jax.experimental.pallas import tpu as pltpu
from jax.sharding import PartitionSpec as P

MESH = pl.DeviceIdType.MESH
W = (-49.0 / 18.0, 1.5, -0.15, 1.0 / 90.0)
DT = 0.1
EARLY, SECOND = 1, 2
VMEM_LIMIT = 44 * 2**20
NZ = 128
STATES = 64
M = 8
ONE, THREE, TWO = 0, 1, 2


def stencil_tables(scale):
    lane = lax.broadcasted_iota(jnp.int32, (8, 128), 1)
    sub = lax.broadcasted_iota(jnp.int32, (8, 128), 0)
    y = lane % 32
    w = [scale * v for v in W]
    cy = {}
    for s in (1, -1, 2, -2, 3, -3):
        cy[s] = jnp.where((y + s >= 0) & (y + s < 32), w[abs(s)], 0.0)
    m32 = jnp.where(lane >= 32, w[1], w[3])
    m96 = jnp.where(lane < 96, w[1], w[3])
    up = [jnp.where((lane < 32 * j) & (sub < 7), w[j], 0.0) for j in (1, 2, 3)]
    down = [jnp.where((lane >= 128 - 32 * j) & (sub > 0), w[j], 0.0) for j in (1, 2, 3)]
    return w, cy, m32, m96, up, down


def laplacian(tables, ref, vol, row):
    w, cy, m32, m96, up, down = tables

    def plane(d):
        return ref[vol, pl.ds(pl.multiple_of(row + 8 * d, 8), 8 * M), :].reshape(M, 8, 128)

    f = plane(0)
    t = (3.0 * w[0]) * f
    for j in (1, 2, 3):
        t = t + w[j] * (plane(-j) + plane(j))
    for s in (1, -1, 2, -2, 3, -3):
        t = t + cy[s] * pltpu.roll(f, (-s) % 128, 2)
    r32, r64, r96 = (pltpu.roll(f, 32 * j, 2) for j in (1, 2, 3))
    t = t + m32 * r32 + w[2] * r64 + m96 * r96
    above = up[0] * r32 + up[1] * r64 + up[2] * r96
    below = down[0] * r96 + down[1] * r64 + down[2] * r32
    return f, t + pltpu.roll(above, 1, 1) + pltpu.roll(below, 7, 1)


def two_thirds(n):
    y = jnp.exp(jnp.log(jnp.maximum(n, 1e-30)) * (1.0 / 3.0))
    y = y - (y * y * y - n) / (3.0 * y * y)
    return y * y


def kernel(shift_in, boost_in, x_ref, o_ref,
           shift_ref, boost_ref, x_buf, land, e_buf, b_buf, p_buf, trig, d1, rs1, t1, swapped, s1, sel1, ag1, f0, acc, d2, rs2, t2, ag2,
           x_sem, slab_send, slab_recv, rs1_send, rs1_recv, swap_sem, s1_send, s1_recv, ag1_send, ag1_recv,
           rs2_send, rs2_recv, ag2_send, ag2_recv, halo_send, halo_recv):
    slabs = lax.axis_size("slab")
    groups = lax.axis_size("grp")
    i = lax.axis_index("slab")
    g = lax.axis_index("grp")
    core = lax.rem(i, 2)
    mate = i + 1 - 2 * core

    def slab(d):
        return (lax.rem(i + d + slabs, slabs), g)

    def peer(k):
        return (i, lax.rem(g + k, groups))

    def own_copy(c):
        return pltpu.make_async_copy(x_ref.at[c], x_buf.at[c], x_sem.at[c])

    own_copy(0).start()
    own_copy(1).start()
    given = [pltpu.make_async_copy(a, b, x_sem.at[2 + n]) for n, (a, b) in enumerate(((shift_in, shift_ref), (boost_in, boost_ref)))]
    for copy in given:
        copy.start()

    barrier = pltpu.get_barrier_semaphore()
    for d in (1, -1, 2, -2, 3, -3):
        pl.semaphore_signal(barrier, inc=1, device_id=slab(d), device_id_type=MESH)

    def greet(k, _):
        pl.semaphore_signal(barrier, inc=1, device_id=peer(k), device_id_type=MESH)
        return 0

    lax.fori_loop(1, groups, greet, 0)

    for c in range(2):
        own_copy(c).wait()

        def relay(m, _):
            s = m // 4
            k = lax.rem(m, 4)
            for j in range(8):
                land[c, s, k, pl.ds(192 - 192 * c + j, 8, stride=8), :] = x_buf[c, s, k, :, 128 * j:128 * j + 128]
            return 0

        lax.fori_loop(0, 16, relay, 0)

        def terms(p, _):
            at = pl.ds(pl.multiple_of(192 - 192 * c + 8 * p, 8), 8)
            n = kr = ki = None
            for s in range(4):
                ur, ui, vr, vi = (land[c, s, k, at, :] for k in range(4))
                a = vr * vr + vi * vi
                b = ur * vr + ui * vi
                e = ui * vr - ur * vi
                n, kr, ki = (a, b, e) if s == 0 else (n + a, kr + b, ki + e)
            for q, v in enumerate((n, kr, ki)):
                d1[p, c, q] = v
            return 0

        lax.fori_loop(0, 8, terms, 0)

    for copy in given:
        copy.wait()

    def phases(m, _):
        c = m // 14
        q = lax.rem(m, 14)
        index = (boost_ref[c] * (8 * i + q - 3)) & (NZ - 1)
        angle = jnp.full((8, 128), index, jnp.int32).astype(jnp.float32) * (2.0 * math.pi / NZ)
        trig[c, q, 0] = jnp.cos(angle)
        trig[c, q, 1] = jnp.sin(angle)
        return 0

    lax.fori_loop(0, 28, phases, 0)
    acc[...] = jnp.zeros_like(acc)

    pl.semaphore_wait(barrier, 6 + groups - 1)

    column = g // 8
    z_own = lax.rem(g, 8)

    def in_group(k):
        return lax.rem(g + k, groups)

    def in_column(k):
        return column * 8 + lax.rem(z_own + k, 8)

    def start(make, count):
        for k in sorted(range(1, count), key=lambda k: -min(k % 8, 8 - k % 8)):
            make(k).start()

    def wait_send(make, count):
        def body(k, _):
            make(k).wait_send()
            return 0
        lax.fori_loop(1, count, body, 0)

    def wait_recv(buf, sem, count, mine):
        def body(k, _):
            o = lax.rem(mine + k, count)
            pltpu.make_async_copy(buf.at[o], buf.at[o], sem.at[o]).wait()
            return 0
        lax.fori_loop(1, count, body, 0)

    def exchange(src, dst, send, recv, one, count, mine):
        def make(k):
            o = lax.rem(mine + k, count)
            to = in_group(k) if count == groups else in_column(k)
            return pltpu.make_async_remote_copy(
                src_ref=src if one else src.at[o], dst_ref=dst.at[mine], send_sem=send.at[o], recv_sem=recv.at[mine],
                device_id=(i, to), device_id_type=MESH)
        return make

    rs1_copy = exchange(d1, rs1, rs1_send, rs1_recv, False, 8, z_own)
    ag1_copy = exchange(sel1, ag1, ag1_send, ag1_recv, True, 8, z_own)
    rs2_copy = exchange(d2, rs2, rs2_send, rs2_recv, False, groups, g)
    ag2_copy = exchange(t2, ag2, ag2_send, ag2_recv, True, groups, g)

    def window(c, s, first, planes):
        return land.at[c, s, :, pl.ds(pl.multiple_of(first * 8, 8), planes * 8)]

    def move(slot, c, s, src, dst, planes, device):
        return pltpu.make_async_remote_copy(
            src_ref=window(c, s, src, planes), dst_ref=window(c, s, dst, planes),
            send_sem=slab_send.at[slot, c, s], recv_sem=slab_recv.at[slot, c, s],
            device_id=device, device_id_type=MESH)

    def far_copy(c, s):
        return move(TWO, c, s, 24 - 24 * c, 8 + 8 * c, 8, slab(2 - 4 * c))

    def near_copy(s):
        return move(ONE, core, s, 24 - 24 * core, 16 - 8 * core, 8, (mate, g))

    def third_copy(s):
        return move(THREE, 1 - core, s, 30 * core, 24 - 18 * core, 2, slab(6 * core - 3))

    def forward_one(s):
        return move(ONE, 1 - core, s, 16 - 8 * core, 8 + 8 * core, 8, (mate, g))

    def forward_three(s):
        return move(THREE, core, s, 14 + 2 * core, 6 + 18 * core, 2, (mate, g))

    def arrived(slot, c, s, planes):
        here = window(c, s, 0, planes)
        pltpu.make_async_copy(here, here, slab_recv.at[slot, c, s]).wait()

    def start_moves(s, _):
        far_copy(0, s).start()
        far_copy(1, s).start()
        near_copy(s).start()
        third_copy(s).start()
        return 0

    def forward(s):
        arrived(TWO, 0, s, 8)
        arrived(TWO, 1, s, 8)
        forward_one(s).start()
        forward_three(s).start()

    start(rs1_copy, 8)
    lax.fori_loop(0, EARLY, start_moves, 0)
    rs1[z_own] = d1[z_own]

    wait_recv(rs1, rs1_recv, 8, z_own)

    def add1(k, total):
        return total + rs1[k]

    t1[...] = lax.fori_loop(1, 8, add1, rs1[0])
    swap = pltpu.make_async_remote_copy(
        src_ref=t1, dst_ref=swapped, send_sem=swap_sem.at[0], recv_sem=swap_sem.at[1],
        device_id=peer(8), device_id_type=MESH)
    swap.start()
    lax.fori_loop(EARLY, SECOND, start_moves, 0)
    swap.wait()
    t1[...] += swapped[...]

    def s1_copy(c, d):
        return pltpu.make_async_remote_copy(
            src_ref=t1.at[c], dst_ref=s1.at[c, d], send_sem=s1_send.at[c, d], recv_sem=s1_recv.at[c, d],
            device_id=slab((1 - 2 * c) * (d + 1)), device_id_type=MESH)

    cases = [(c, d) for c in range(2) for d in range(2)]
    for case in cases:
        s1_copy(*case).start()
    lax.fori_loop(SECOND, 4, start_moves, 0)
    forward(0)
    for case in cases:
        s1_copy(*case).wait_recv()
    r0 = shift_ref[0] - 8
    r1 = shift_ref[1] - 8
    from_0 = ((z_own + r0) >> 3) & 1
    from_1 = ((7 - z_own + r1) >> 3) & 1
    sel1[0] = s1[0, from_0]
    sel1[1] = s1[1, from_1]
    start(ag1_copy, 8)
    ag1[z_own] = sel1[...]
    forward(1)
    wait_recv(ag1, ag1_recv, 8, z_own)

    def fields_now(p, _):
        n = kr = ki = None
        for c in range(2):
            src = (p - r0 if c == 0 else p + r1) & 7
            cos, sin = trig[c, p + 3, 0], trig[c, p + 3, 1]
            cos, sin = cos * cos - sin * sin, 2.0 * cos * sin
            a, b, e = ag1[src, c, 0], ag1[src, c, 1], ag1[src, c, 2]
            b, e = b * cos - e * sin, b * sin + e * cos
            n, kr, ki = (a, b, e) if c == 0 else (n + a, kr + b, ki + e)
        f0[0, p] = DT * (1.2 * two_thirds(n * (1.0 / STATES)) - 1.0)
        f0[1, p] = kr * (-3.0 * DT / STATES)
        f0[2, p] = ki * (-3.0 * DT / STATES)
        return 0

    lax.fori_loop(0, 8, fields_now, 0)

    tables = stencil_tables(0.5 * DT)

    def halo_copy(d, s):
        src = pl.ds(24, 24) if d == 0 else pl.ds(64, 24)
        dst = pl.ds(88, 24) if d == 0 else pl.ds(0, 24)
        vols = pl.ds(s * 8, 8)
        return pltpu.make_async_remote_copy(
            src_ref=p_buf.at[vols, src], dst_ref=p_buf.at[vols, dst],
            send_sem=halo_send.at[d, s], recv_sem=halo_recv.at[d, s],
            device_id=slab(2 * d - 1), device_id_type=MESH)

    def send_halos(s):
        halo_copy(0, s).start()
        halo_copy(1, s).start()

    def state_step(s, _):
        for c in range(2):
            arrived(ONE, c, s, 8)
            arrived(THREE, c, s, 2)
            for k in range(4):
                e_buf[k] = land[c, s, k, 48:208, :].reshape(20, 8, 128)
            vol = (s * 2 + c) * 4
            base = 7 - r0 if c == 0 else r1 - 1

            def boost(q, _):
                cos, sin = trig[c, q, 0], trig[c, q, 1]
                plane = jnp.maximum(jnp.minimum(base + q, 19), 0)
                ur, ui, vr, vi = (e_buf[k, plane] for k in range(4))
                to = pl.ds(pl.multiple_of(q * 8, 8), 8)
                b_buf[vol, to, :] = ur * cos - ui * sin
                b_buf[vol + 1, to, :] = ur * sin + ui * cos
                b_buf[vol + 2, to, :] = vr * cos + vi * sin
                b_buf[vol + 3, to, :] = vi * cos - vr * sin
                return 0

            lax.fori_loop(0, 14, boost, 0)

            def predict(m, _):
                p = m * M
                row = pl.multiple_of((p + 3) * 8, 8)
                pot, dr, di = (f0[q, pl.ds(p, M)] for q in range(3))
                ur, lur = laplacian(tables, b_buf, vol, row)
                ui, lui = laplacian(tables, b_buf, vol + 1, row)
                vr, lvr = laplacian(tables, b_buf, vol + 2, row)
                vi, lvi = laplacian(tables, b_buf, vol + 3, row)
                pur = ur - lui + (pot * ui + dr * vi + di * vr)
                pui = ui + lur - (pot * ur + dr * vr - di * vi)
                pvr = vr + lvi + (dr * ui - di * ur - pot * vi)
                pvi = vi - lvr - (dr * ur + di * ui - pot * vr)
                at = pl.ds(row, 8 * M)
                for k, v in enumerate((pur, pui, pvr, pvi)):
                    p_buf[vol + k, at, :] = v.reshape(8 * M, 128)
                acc[0, pl.ds(p, M)] += pvr * pvr + pvi * pvi
                acc[1, pl.ds(p, M)] += pur * pvr + pui * pvi
                acc[2, pl.ds(p, M)] += pui * pvr - pur * pvi
                return 0

            lax.fori_loop(0, 8 // M, predict, 0)

        @pl.when(s < 2)
        def _():
            forward(s + 2)

        @pl.when(s == 1)
        def _():
            send_halos(0)
            send_halos(1)

        @pl.when(s == 2)
        def _():
            send_halos(2)

        return 0

    lax.fori_loop(0, 4, state_step, 0)

    for p in range(8):
        for q in range(3):
            v = acc[q, p]
            d2[p, q] = v[0:4]
            d2[8 + p, q] = v[4:8]

    start(rs2_copy, groups)
    send_halos(3)
    rs2[g] = d2[g]
    wait_recv(rs2, rs2_recv, groups, g)

    def add2(k, total):
        return total + rs2[k]

    n, kr, ki = lax.fori_loop(1, groups, add2, rs2[0])
    t2[0] = DT * (1.2 * two_thirds(n * (1.0 / STATES)) - 1.0)
    t2[1] = kr * (-3.0 * DT / STATES)
    t2[2] = ki * (-3.0 * DT / STATES)
    start(ag2_copy, groups)
    ag2[g] = t2[...]

    def kinetic_state(s, _):
        halo_copy(0, s).wait_recv()
        halo_copy(1, s).wait_recv()

        def kinetic(m, _):
            vol = (s * 2 + m // (8 // M)) * 4
            row = pl.multiple_of((lax.rem(m, 8 // M) * M + 3) * 8, 8)
            at = pl.ds(row, 8 * M)
            ur, lur = laplacian(tables, p_buf, vol, row)
            ui, lui = laplacian(tables, p_buf, vol + 1, row)
            vr, lvr = laplacian(tables, p_buf, vol + 2, row)
            vi, lvi = laplacian(tables, p_buf, vol + 3, row)
            for k, v in enumerate((ur - lui, ui + lur, vr + lvi, vi - lvr)):
                b_buf[vol + k, at, :] += v.reshape(8 * M, 128)
            return 0

        lax.fori_loop(0, 16 // M, kinetic, 0)
        return 0

    lax.fori_loop(0, 4, kinetic_state, 0)
    wait_recv(ag2, ag2_recv, groups, g)

    def correct(p, _):
        pot, dr, di = (jnp.concatenate([ag2[p, q], ag2[8 + p, q]], axis=0) for q in range(3))
        at = pl.ds(pl.multiple_of((p + 3) * 8, 8), 8)
        to = pl.ds(p, 8, stride=8)
        for s in range(4):
            for c in range(2):
                vol = (s * 2 + c) * 4
                out = (c * 4 + s) * 4
                ur, ui, vr, vi = (p_buf[vol + k, at, :] for k in range(4))
                gur, gui, gvr, gvi = (b_buf[vol + k, at, :] for k in range(4))
                o_ref[out, to, :] = 0.5 * (gur + (pot * ui + dr * vi + di * vr))
                o_ref[out + 1, to, :] = 0.5 * (gui - (pot * ur + dr * vr - di * vi))
                o_ref[out + 2, to, :] = 0.5 * (gvr + (dr * ui - di * ur - pot * vi))
                o_ref[out + 3, to, :] = 0.5 * (gvi - (dr * ur + di * ui - pot * vr))
        return 0

    lax.fori_loop(0, 8, correct, 0)

    wait_send(rs1_copy, 8)
    wait_send(ag1_copy, 8)
    wait_send(rs2_copy, groups)
    wait_send(ag2_copy, groups)
    for case in cases:
        s1_copy(*case).wait_send()

    def moves_sent(s, _):
        for c in range(2):
            far_copy(c, s).wait_send()
            halo_copy(c, s).wait_send()
        near_copy(s).wait_send()
        third_copy(s).wait_send()
        forward_one(s).wait_send()
        forward_three(s).wait_send()
        return 0

    lax.fori_loop(0, 4, moves_sent, 0)


def local(cloud_states, cloud_shift, boost_wave):
    f32 = jnp.float32
    hbm = pl.BlockSpec(memory_space=pltpu.HBM)
    operands = [pltpu.with_memory_space_constraint(a, pltpu.HBM) for a in (cloud_shift, boost_wave, cloud_states)]
    dma = pltpu.SemaphoreType.DMA
    out = pl.pallas_call(
        kernel,
        out_shape=jax.ShapeDtypeStruct((32, 64, 128), f32),
        in_specs=[hbm, hbm, hbm],
        out_specs=pl.BlockSpec(memory_space=pltpu.VMEM),
        scratch_shapes=[
            pltpu.SMEM((2,), jnp.int32),
            pltpu.SMEM((2,), jnp.int32),
            pltpu.VMEM((2, 4, 4, 8, 1024), f32),
            pltpu.VMEM((2, 4, 4, 256, 128), f32),
            pltpu.VMEM((4, 20, 8, 128), f32),
            pltpu.VMEM((32, 112, 128), f32),
            pltpu.VMEM((32, 112, 128), f32),
            pltpu.VMEM((2, 14, 2, 8, 128), f32),
            pltpu.VMEM((8, 2, 3, 8, 128), f32),
            pltpu.VMEM((8, 2, 3, 8, 128), f32),
            pltpu.VMEM((2, 3, 8, 128), f32),
            pltpu.VMEM((2, 3, 8, 128), f32),
            pltpu.VMEM((2, 2, 3, 8, 128), f32),
            pltpu.VMEM((2, 3, 8, 128), f32),
            pltpu.VMEM((8, 2, 3, 8, 128), f32),
            pltpu.VMEM((3, 8, 8, 128), f32),
            pltpu.VMEM((3, 8, 8, 128), f32),
            pltpu.VMEM((16, 3, 4, 128), f32),
            pltpu.VMEM((16, 3, 4, 128), f32),
            pltpu.VMEM((3, 4, 128), f32),
            pltpu.VMEM((16, 3, 4, 128), f32),
            dma((4,)), dma((3, 2, 4)), dma((3, 2, 4)),
            dma((8,)), dma((8,)), dma((2,)), dma((2, 2)), dma((2, 2)), dma((8,)), dma((8,)),
            dma((16,)), dma((16,)), dma((16,)), dma((16,)), dma((2, 4)), dma((2, 4)),
        ],
        compiler_params=pltpu.CompilerParams(
            collective_id=0, has_side_effects=True, vmem_limit_bytes=VMEM_LIMIT),
    )(*operands)
    out = out.reshape(2, 4, 4, 8, 8, 128).transpose(0, 1, 2, 4, 3, 5)
    return out.reshape(2, 4, 4, 8, 1024)


def solution(mesh):
    in_specs = (P(None, "grp", None, "slab", None), P(), P())
    out_specs = P(None, "grp", None, "slab", None)
    return jax.shard_map(local, mesh=mesh, in_specs=in_specs, out_specs=out_specs, check_vma=False)
```

```python
import math

import jax
import jax.numpy as jnp
from jax import lax
from jax.experimental import pallas as pl
from jax.experimental.pallas import tpu as pltpu
from jax.sharding import PartitionSpec as P

MESH = pl.DeviceIdType.MESH
W = (-49.0 / 18.0, 1.5, -0.15, 1.0 / 90.0)
DT = 0.1
EARLY, SECOND = 1, 2
VMEM_LIMIT = 44 * 2**20
NZ = 128
STATES = 64
M = 8
ONE, THREE, TWO, EDGE, REST = range(5)


def stencil_tables(scale):
    lane = lax.broadcasted_iota(jnp.int32, (8, 128), 1)
    sub = lax.broadcasted_iota(jnp.int32, (8, 128), 0)
    y = lane % 32
    w = [scale * v for v in W]
    cy = {}
    for s in (1, -1, 2, -2, 3, -3):
        cy[s] = jnp.where((y + s >= 0) & (y + s < 32), w[abs(s)], 0.0)
    m32 = jnp.where(lane >= 32, w[1], w[3])
    m96 = jnp.where(lane < 96, w[1], w[3])
    up = [jnp.where((lane < 32 * j) & (sub < 7), w[j], 0.0) for j in (1, 2, 3)]
    down = [jnp.where((lane >= 128 - 32 * j) & (sub > 0), w[j], 0.0) for j in (1, 2, 3)]
    return w, cy, m32, m96, up, down


def laplacian(tables, ref, vol, row):
    w, cy, m32, m96, up, down = tables

    def plane(d):
        return ref[vol, pl.ds(pl.multiple_of(row + 8 * d, 8), 8 * M), :].reshape(M, 8, 128)

    f = plane(0)
    t = (3.0 * w[0]) * f
    for j in (1, 2, 3):
        t = t + w[j] * (plane(-j) + plane(j))
    for s in (1, -1, 2, -2, 3, -3):
        t = t + cy[s] * pltpu.roll(f, (-s) % 128, 2)
    r32, r64, r96 = (pltpu.roll(f, 32 * j, 2) for j in (1, 2, 3))
    t = t + m32 * r32 + w[2] * r64 + m96 * r96
    above = up[0] * r32 + up[1] * r64 + up[2] * r96
    below = down[0] * r96 + down[1] * r64 + down[2] * r32
    return f, t + pltpu.roll(above, 1, 1) + pltpu.roll(below, 7, 1)


def two_thirds(n):
    y = jnp.exp(jnp.log(jnp.maximum(n, 1e-30)) * (1.0 / 3.0))
    y = y - (y * y * y - n) / (3.0 * y * y)
    return y * y


def kernel(shift_in, boost_in, x_ref, o_ref,
           shift_ref, boost_ref, x_buf, land, e_buf, b_buf, p_buf, trig, d1, rs1, t1, swapped, s1, sel1, ag1, f0, acc, d2, rs2, t2, ag2,
           x_sem, slab_send, slab_recv, rs1_send, rs1_recv, swap_sem, s1_send, s1_recv, ag1_send, ag1_recv,
           rs2_send, rs2_recv, ag2_send, ag2_recv, halo_send, halo_recv):
    slabs = lax.axis_size("slab")
    groups = lax.axis_size("grp")
    i = lax.axis_index("slab")
    g = lax.axis_index("grp")
    core = lax.rem(i, 2)
    mate = i + 1 - 2 * core

    def slab(d):
        return (lax.rem(i + d + slabs, slabs), g)

    def peer(k):
        return (i, lax.rem(g + k, groups))

    def own_copy(c):
        return pltpu.make_async_copy(x_ref.at[c], x_buf.at[c], x_sem.at[c])

    own_copy(0).start()
    own_copy(1).start()
    given = [pltpu.make_async_copy(a, b, x_sem.at[2 + n]) for n, (a, b) in enumerate(((shift_in, shift_ref), (boost_in, boost_ref)))]
    for copy in given:
        copy.start()

    barrier = pltpu.get_barrier_semaphore()
    for d in (1, -1, 2, -2, 3, -3):
        pl.semaphore_signal(barrier, inc=1, device_id=slab(d), device_id_type=MESH)

    def greet(k, _):
        pl.semaphore_signal(barrier, inc=1, device_id=peer(k), device_id_type=MESH)
        return 0

    lax.fori_loop(1, groups, greet, 0)

    for c in range(2):
        own_copy(c).wait()

        def relay(m, _):
            s = m // 4
            k = lax.rem(m, 4)
            for j in range(8):
                land[c, s, k, pl.ds(192 - 192 * c + j, 8, stride=8), :] = x_buf[c, s, k, :, 128 * j:128 * j + 128]
            return 0

        lax.fori_loop(0, 16, relay, 0)

        def terms(p, _):
            at = pl.ds(pl.multiple_of(192 - 192 * c + 8 * p, 8), 8)
            n = kr = ki = None
            for s in range(4):
                ur, ui, vr, vi = (land[c, s, k, at, :] for k in range(4))
                a = vr * vr + vi * vi
                b = ur * vr + ui * vi
                e = ui * vr - ur * vi
                n, kr, ki = (a, b, e) if s == 0 else (n + a, kr + b, ki + e)
            for q, v in enumerate((n, kr, ki)):
                d1[p, c, q] = v
            return 0

        lax.fori_loop(0, 8, terms, 0)

    for copy in given:
        copy.wait()

    def phases(m, _):
        c = m // 14
        q = lax.rem(m, 14)
        index = (boost_ref[c] * (8 * i + q - 3)) & (NZ - 1)
        angle = jnp.full((8, 128), index, jnp.int32).astype(jnp.float32) * (2.0 * math.pi / NZ)
        trig[c, q, 0] = jnp.cos(angle)
        trig[c, q, 1] = jnp.sin(angle)
        return 0

    lax.fori_loop(0, 28, phases, 0)
    acc[...] = jnp.zeros_like(acc)

    pl.semaphore_wait(barrier, 6 + groups - 1)

    column = g // 8
    z_own = lax.rem(g, 8)

    def in_group(k):
        return lax.rem(g + k, groups)

    def in_column(k):
        return column * 8 + lax.rem(z_own + k, 8)

    def start(make, count):
        for k in sorted(range(1, count), key=lambda k: -min(k % 8, 8 - k % 8)):
            make(k).start()

    def wait_send(make, count):
        def body(k, _):
            make(k).wait_send()
            return 0
        lax.fori_loop(1, count, body, 0)

    def wait_recv(buf, sem, count, mine):
        def body(k, _):
            o = lax.rem(mine + k, count)
            pltpu.make_async_copy(buf.at[o], buf.at[o], sem.at[o]).wait()
            return 0
        lax.fori_loop(1, count, body, 0)

    def exchange(src, dst, send, recv, one, count, mine):
        def make(k):
            o = lax.rem(mine + k, count)
            to = in_group(k) if count == groups else in_column(k)
            return pltpu.make_async_remote_copy(
                src_ref=src if one else src.at[o], dst_ref=dst.at[mine], send_sem=send.at[o], recv_sem=recv.at[mine],
                device_id=(i, to), device_id_type=MESH)
        return make

    rs1_copy = exchange(d1, rs1, rs1_send, rs1_recv, False, 8, z_own)
    ag1_copy = exchange(sel1, ag1, ag1_send, ag1_recv, True, 8, z_own)
    rs2_copy = exchange(d2, rs2, rs2_send, rs2_recv, False, groups, g)
    ag2_copy = exchange(t2, ag2, ag2_send, ag2_recv, True, groups, g)

    def window(c, s, first, planes):
        return land.at[c, s, :, pl.ds(pl.multiple_of(first * 8, 8), planes * 8)]

    def move(slot, c, s, src, dst, planes, device):
        return pltpu.make_async_remote_copy(
            src_ref=window(c, s, src, planes), dst_ref=window(c, s, dst, planes),
            send_sem=slab_send.at[slot, c, s], recv_sem=slab_recv.at[slot, c, s],
            device_id=device, device_id_type=MESH)

    def far_copy(c, s):
        return move(TWO, c, s, 24 - 24 * c, 8 + 8 * c, 8, slab(2 - 4 * c))

    def last_copies():
        to = slab(2 - 4 * core), slab(4 * core - 2)
        return (move(TWO, 1 - core, 3, 24 * core, 16 - 8 * core, 8, to[1]),
                move(EDGE, core, 3, 30 - 30 * core, 14 + 2 * core, 2, to[0]),
                move(REST, core, 3, 24 - 22 * core, 8 + 10 * core, 6, to[0]))

    def near_copy(s):
        return move(ONE, core, s, 24 - 24 * core, 16 - 8 * core, 8, (mate, g))

    def third_copy(s):
        return move(THREE, 1 - core, s, 30 * core, 24 - 18 * core, 2, slab(6 * core - 3))

    def forward_one(s):
        return move(ONE, 1 - core, s, 16 - 8 * core, 8 + 8 * core, 8, (mate, g))

    def forward_three(s):
        return move(THREE, core, s, 14 + 2 * core, 6 + 18 * core, 2, (mate, g))

    def arrived(slot, c, s, planes):
        here = window(c, s, 0, planes)
        pltpu.make_async_copy(here, here, slab_recv.at[slot, c, s]).wait()

    def start_moves(s):
        for copy in last_copies() if s == 3 else (far_copy(0, s), far_copy(1, s)):
            copy.start()
        near_copy(s).start()
        third_copy(s).start()

    def forward(s):
        arrived(TWO, 0, s, 8)
        arrived(TWO, 1, s, 8)
        forward_one(s).start()
        forward_three(s).start()

    def forward_last():
        arrived(TWO, 1 - core, 3, 8)
        forward_one(3).start()
        arrived(EDGE, core, 3, 2)
        forward_three(3).start()

    start(rs1_copy, 8)
    for s in range(EARLY):
        start_moves(s)
    rs1[z_own] = d1[z_own]

    wait_recv(rs1, rs1_recv, 8, z_own)

    def add1(k, total):
        return total + rs1[k]

    t1[...] = lax.fori_loop(1, 8, add1, rs1[0])
    swap = pltpu.make_async_remote_copy(
        src_ref=t1, dst_ref=swapped, send_sem=swap_sem.at[0], recv_sem=swap_sem.at[1],
        device_id=peer(8), device_id_type=MESH)
    swap.start()
    for s in range(EARLY, SECOND):
        start_moves(s)
    swap.wait()
    t1[...] += swapped[...]

    def s1_copy(c, d):
        return pltpu.make_async_remote_copy(
            src_ref=t1.at[c], dst_ref=s1.at[c, d], send_sem=s1_send.at[c, d], recv_sem=s1_recv.at[c, d],
            device_id=slab((1 - 2 * c) * (d + 1)), device_id_type=MESH)

    cases = [(c, d) for c in range(2) for d in range(2)]
    for case in cases:
        s1_copy(*case).start()
    for s in range(SECOND, 4):
        start_moves(s)
    forward(0)
    for case in cases:
        s1_copy(*case).wait_recv()
    r0 = shift_ref[0] - 8
    r1 = shift_ref[1] - 8
    from_0 = ((z_own + r0) >> 3) & 1
    from_1 = ((7 - z_own + r1) >> 3) & 1
    sel1[0] = s1[0, from_0]
    sel1[1] = s1[1, from_1]
    start(ag1_copy, 8)
    ag1[z_own] = sel1[...]
    forward(1)
    wait_recv(ag1, ag1_recv, 8, z_own)

    def fields_now(p, _):
        n = kr = ki = None
        for c in range(2):
            src = (p - r0 if c == 0 else p + r1) & 7
            cos, sin = trig[c, p + 3, 0], trig[c, p + 3, 1]
            cos, sin = cos * cos - sin * sin, 2.0 * cos * sin
            a, b, e = ag1[src, c, 0], ag1[src, c, 1], ag1[src, c, 2]
            b, e = b * cos - e * sin, b * sin + e * cos
            n, kr, ki = (a, b, e) if c == 0 else (n + a, kr + b, ki + e)
        f0[0, p] = DT * (1.2 * two_thirds(n * (1.0 / STATES)) - 1.0)
        f0[1, p] = kr * (-3.0 * DT / STATES)
        f0[2, p] = ki * (-3.0 * DT / STATES)
        return 0

    lax.fori_loop(0, 8, fields_now, 0)

    tables = stencil_tables(0.5 * DT)

    def halo_copy(d, s):
        src = pl.ds(24, 24) if d == 0 else pl.ds(64, 24)
        dst = pl.ds(88, 24) if d == 0 else pl.ds(0, 24)
        vols = pl.ds(s * 8, 8)
        return pltpu.make_async_remote_copy(
            src_ref=p_buf.at[vols, src], dst_ref=p_buf.at[vols, dst],
            send_sem=halo_send.at[d, s], recv_sem=halo_recv.at[d, s],
            device_id=slab(2 * d - 1), device_id_type=MESH)

    def send_halos(s):
        halo_copy(0, s).start()
        halo_copy(1, s).start()

    def state_step(s, _):
        for c in range(2):
            arrived(ONE, c, s, 8)
            arrived(THREE, c, s, 2)
            for k in range(4):
                e_buf[k] = land[c, s, k, 48:208, :].reshape(20, 8, 128)
            vol = (s * 2 + c) * 4
            base = 7 - r0 if c == 0 else r1 - 1

            def boost(q, _):
                cos, sin = trig[c, q, 0], trig[c, q, 1]
                plane = jnp.maximum(jnp.minimum(base + q, 19), 0)
                ur, ui, vr, vi = (e_buf[k, plane] for k in range(4))
                to = pl.ds(pl.multiple_of(q * 8, 8), 8)
                b_buf[vol, to, :] = ur * cos - ui * sin
                b_buf[vol + 1, to, :] = ur * sin + ui * cos
                b_buf[vol + 2, to, :] = vr * cos + vi * sin
                b_buf[vol + 3, to, :] = vi * cos - vr * sin
                return 0

            lax.fori_loop(0, 14, boost, 0)

            def predict(m, _):
                p = m * M
                row = pl.multiple_of((p + 3) * 8, 8)
                pot, dr, di = (f0[q, pl.ds(p, M)] for q in range(3))
                ur, lur = laplacian(tables, b_buf, vol, row)
                ui, lui = laplacian(tables, b_buf, vol + 1, row)
                vr, lvr = laplacian(tables, b_buf, vol + 2, row)
                vi, lvi = laplacian(tables, b_buf, vol + 3, row)
                pur = ur - lui + (pot * ui + dr * vi + di * vr)
                pui = ui + lur - (pot * ur + dr * vr - di * vi)
                pvr = vr + lvi + (dr * ui - di * ur - pot * vi)
                pvi = vi - lvr - (dr * ur + di * ui - pot * vr)
                at = pl.ds(row, 8 * M)
                for k, v in enumerate((pur, pui, pvr, pvi)):
                    p_buf[vol + k, at, :] = v.reshape(8 * M, 128)
                acc[0, pl.ds(p, M)] += pvr * pvr + pvi * pvi
                acc[1, pl.ds(p, M)] += pur * pvr + pui * pvi
                acc[2, pl.ds(p, M)] += pui * pvr - pur * pvi
                return 0

            lax.fori_loop(0, 8 // M, predict, 0)

        @pl.when(s == 0)
        def _():
            forward(2)

        @pl.when(s == 1)
        def _():
            forward_last()

        @pl.when(s < 3)
        def _():
            send_halos(s)

        @pl.when(s == 2)
        def _():
            arrived(REST, core, 3, 6)

        return 0

    lax.fori_loop(0, 4, state_step, 0)

    for p in range(8):
        for q in range(3):
            v = acc[q, p]
            d2[p, q] = v[0:4]
            d2[8 + p, q] = v[4:8]

    start(rs2_copy, groups)
    send_halos(3)
    rs2[g] = d2[g]
    wait_recv(rs2, rs2_recv, groups, g)

    def add2(k, total):
        return total + rs2[k]

    n, kr, ki = lax.fori_loop(1, groups, add2, rs2[0])
    t2[0] = DT * (1.2 * two_thirds(n * (1.0 / STATES)) - 1.0)
    t2[1] = kr * (-3.0 * DT / STATES)
    t2[2] = ki * (-3.0 * DT / STATES)
    start(ag2_copy, groups)
    ag2[g] = t2[...]

    def kinetic_state(s, _):
        halo_copy(0, s).wait_recv()
        halo_copy(1, s).wait_recv()

        def kinetic(m, _):
            vol = (s * 2 + m // (8 // M)) * 4
            row = pl.multiple_of((lax.rem(m, 8 // M) * M + 3) * 8, 8)
            at = pl.ds(row, 8 * M)
            ur, lur = laplacian(tables, p_buf, vol, row)
            ui, lui = laplacian(tables, p_buf, vol + 1, row)
            vr, lvr = laplacian(tables, p_buf, vol + 2, row)
            vi, lvi = laplacian(tables, p_buf, vol + 3, row)
            for k, v in enumerate((ur - lui, ui + lur, vr + lvi, vi - lvr)):
                b_buf[vol + k, at, :] += v.reshape(8 * M, 128)
            return 0

        lax.fori_loop(0, 16 // M, kinetic, 0)
        return 0

    lax.fori_loop(0, 4, kinetic_state, 0)
    wait_recv(ag2, ag2_recv, groups, g)

    def correct(p, _):
        pot, dr, di = (jnp.concatenate([ag2[p, q], ag2[8 + p, q]], axis=0) for q in range(3))
        at = pl.ds(pl.multiple_of((p + 3) * 8, 8), 8)
        to = pl.ds(p, 8, stride=8)
        for s in range(4):
            for c in range(2):
                vol = (s * 2 + c) * 4
                out = (c * 4 + s) * 4
                ur, ui, vr, vi = (p_buf[vol + k, at, :] for k in range(4))
                gur, gui, gvr, gvi = (b_buf[vol + k, at, :] for k in range(4))
                o_ref[out, to, :] = 0.5 * (gur + (pot * ui + dr * vi + di * vr))
                o_ref[out + 1, to, :] = 0.5 * (gui - (pot * ur + dr * vr - di * vi))
                o_ref[out + 2, to, :] = 0.5 * (gvr + (dr * ui - di * ur - pot * vi))
                o_ref[out + 3, to, :] = 0.5 * (gvi - (dr * ur + di * ui - pot * vr))
        return 0

    lax.fori_loop(0, 8, correct, 0)

    wait_send(rs1_copy, 8)
    wait_send(ag1_copy, 8)
    wait_send(rs2_copy, groups)
    wait_send(ag2_copy, groups)
    for case in cases:
        s1_copy(*case).wait_send()

    def moves_sent(s, _):
        for c in range(2):
            halo_copy(c, s).wait_send()
        near_copy(s).wait_send()
        third_copy(s).wait_send()
        forward_one(s).wait_send()
        forward_three(s).wait_send()
        return 0

    lax.fori_loop(0, 4, moves_sent, 0)
    for s in range(4):
        for copy in last_copies() if s == 3 else (far_copy(0, s), far_copy(1, s)):
            copy.wait_send()


def local(cloud_states, cloud_shift, boost_wave):
    f32 = jnp.float32
    hbm = pl.BlockSpec(memory_space=pltpu.HBM)
    operands = [pltpu.with_memory_space_constraint(a, pltpu.HBM) for a in (cloud_shift, boost_wave, cloud_states)]
    dma = pltpu.SemaphoreType.DMA
    out = pl.pallas_call(
        kernel,
        out_shape=jax.ShapeDtypeStruct((32, 64, 128), f32),
        in_specs=[hbm, hbm, hbm],
        out_specs=pl.BlockSpec(memory_space=pltpu.VMEM),
        scratch_shapes=[
            pltpu.SMEM((2,), jnp.int32),
            pltpu.SMEM((2,), jnp.int32),
            pltpu.VMEM((2, 4, 4, 8, 1024), f32),
            pltpu.VMEM((2, 4, 4, 256, 128), f32),
            pltpu.VMEM((4, 20, 8, 128), f32),
            pltpu.VMEM((32, 112, 128), f32),
            pltpu.VMEM((32, 112, 128), f32),
            pltpu.VMEM((2, 14, 2, 8, 128), f32),
            pltpu.VMEM((8, 2, 3, 8, 128), f32),
            pltpu.VMEM((8, 2, 3, 8, 128), f32),
            pltpu.VMEM((2, 3, 8, 128), f32),
            pltpu.VMEM((2, 3, 8, 128), f32),
            pltpu.VMEM((2, 2, 3, 8, 128), f32),
            pltpu.VMEM((2, 3, 8, 128), f32),
            pltpu.VMEM((8, 2, 3, 8, 128), f32),
            pltpu.VMEM((3, 8, 8, 128), f32),
            pltpu.VMEM((3, 8, 8, 128), f32),
            pltpu.VMEM((16, 3, 4, 128), f32),
            pltpu.VMEM((16, 3, 4, 128), f32),
            pltpu.VMEM((3, 4, 128), f32),
            pltpu.VMEM((16, 3, 4, 128), f32),
            dma((4,)), dma((5, 2, 4)), dma((5, 2, 4)),
            dma((8,)), dma((8,)), dma((2,)), dma((2, 2)), dma((2, 2)), dma((8,)), dma((8,)),
            dma((16,)), dma((16,)), dma((16,)), dma((16,)), dma((2, 4)), dma((2, 4)),
        ],
        compiler_params=pltpu.CompilerParams(
            collective_id=0, has_side_effects=True, vmem_limit_bytes=VMEM_LIMIT),
    )(*operands)
    out = out.reshape(2, 4, 4, 8, 8, 128).transpose(0, 1, 2, 4, 3, 5)
    return out.reshape(2, 4, 4, 8, 1024)


def solution(mesh):
    in_specs = (P(None, "grp", None, "slab", None), P(), P())
    out_specs = P(None, "grp", None, "slab", None)
    return jax.shard_map(local, mesh=mesh, in_specs=in_specs, out_specs=out_specs, check_vma=False)
```

```python
import math

import jax
import jax.numpy as jnp
from jax import lax
from jax.experimental import pallas as pl
from jax.experimental.pallas import tpu as pltpu
from jax.sharding import PartitionSpec as P

MESH = pl.DeviceIdType.MESH
W = (-49.0 / 18.0, 1.5, -0.15, 1.0 / 90.0)
DT = 0.1
EARLY, SECOND = 1, 2
VMEM_LIMIT = 44 * 2**20
NZ = 128
STATES = 64
M = 8
ONE, THREE, TWO, EDGE, REST = range(5)


def stencil_tables(scale):
    lane = lax.broadcasted_iota(jnp.int32, (8, 128), 1)
    sub = lax.broadcasted_iota(jnp.int32, (8, 128), 0)
    y = lane % 32
    w = [scale * v for v in W]
    cy = {}
    for s in (1, -1, 2, -2, 3, -3):
        cy[s] = jnp.where((y + s >= 0) & (y + s < 32), w[abs(s)], 0.0)
    m32 = jnp.where(lane >= 32, w[1], w[3])
    m96 = jnp.where(lane < 96, w[1], w[3])
    up = [jnp.where((lane < 32 * j) & (sub < 7), w[j], 0.0) for j in (1, 2, 3)]
    down = [jnp.where((lane >= 128 - 32 * j) & (sub > 0), w[j], 0.0) for j in (1, 2, 3)]
    return w, cy, m32, m96, up, down


def laplacian(tables, ref, vol, row):
    w, cy, m32, m96, up, down = tables

    def plane(d):
        return ref[vol, pl.ds(pl.multiple_of(row + 8 * d, 8), 8 * M), :].reshape(M, 8, 128)

    f = plane(0)
    t = (3.0 * w[0]) * f
    for j in (1, 2, 3):
        t = t + w[j] * (plane(-j) + plane(j))
    for s in (1, -1, 2, -2, 3, -3):
        t = t + cy[s] * pltpu.roll(f, (-s) % 128, 2)
    r32, r64, r96 = (pltpu.roll(f, 32 * j, 2) for j in (1, 2, 3))
    t = t + m32 * r32 + w[2] * r64 + m96 * r96
    above = up[0] * r32 + up[1] * r64 + up[2] * r96
    below = down[0] * r96 + down[1] * r64 + down[2] * r32
    return f, t + pltpu.roll(above, 1, 1) + pltpu.roll(below, 7, 1)


def two_thirds(n):
    y = jnp.exp(jnp.log(jnp.maximum(n, 1e-30)) * (1.0 / 3.0))
    y = y - (y * y * y - n) / (3.0 * y * y)
    return y * y


def kernel(shift_in, boost_in, x_ref, o_ref,
           shift_ref, boost_ref, x_buf, land, e_buf, b_buf, p_buf, h_buf, trig, d1, rs1, t1, swapped, s1, sel1, ag1, f0, acc, d2, rs2, t2, ag2,
           x_sem, slab_send, slab_recv, rs1_send, rs1_recv, swap_sem, s1_send, s1_recv, ag1_send, ag1_recv,
           rs2_send, rs2_recv, ag2_send, ag2_recv, halo_send, halo_recv):
    slabs = lax.axis_size("slab")
    groups = lax.axis_size("grp")
    i = lax.axis_index("slab")
    g = lax.axis_index("grp")
    core = lax.rem(i, 2)
    mate = i + 1 - 2 * core

    def slab(d):
        return (lax.rem(i + d + slabs, slabs), g)

    def peer(k):
        return (i, lax.rem(g + k, groups))

    def own_copy(c):
        return pltpu.make_async_copy(x_ref.at[c], x_buf.at[c], x_sem.at[c])

    own_copy(0).start()
    own_copy(1).start()
    given = [pltpu.make_async_copy(a, b, x_sem.at[2 + n]) for n, (a, b) in enumerate(((shift_in, shift_ref), (boost_in, boost_ref)))]
    for copy in given:
        copy.start()

    barrier = pltpu.get_barrier_semaphore()
    for d in (1, -1, 2, -2, 3, -3):
        pl.semaphore_signal(barrier, inc=1, device_id=slab(d), device_id_type=MESH)

    def greet(k, _):
        pl.semaphore_signal(barrier, inc=1, device_id=peer(k), device_id_type=MESH)
        return 0

    lax.fori_loop(1, groups, greet, 0)

    for c in range(2):
        own_copy(c).wait()

        def relay(m, _):
            s = m // 4
            k = lax.rem(m, 4)
            for j in range(8):
                land[c, s, k, pl.ds(192 - 192 * c + j, 8, stride=8), :] = x_buf[c, s, k, :, 128 * j:128 * j + 128]
            return 0

        lax.fori_loop(0, 16, relay, 0)

        def terms(p, _):
            at = pl.ds(pl.multiple_of(192 - 192 * c + 8 * p, 8), 8)
            n = kr = ki = None
            for s in range(4):
                ur, ui, vr, vi = (land[c, s, k, at, :] for k in range(4))
                a = vr * vr + vi * vi
                b = ur * vr + ui * vi
                e = ui * vr - ur * vi
                n, kr, ki = (a, b, e) if s == 0 else (n + a, kr + b, ki + e)
            for q, v in enumerate((n, kr, ki)):
                d1[p, c, q] = v
            return 0

        lax.fori_loop(0, 8, terms, 0)

    for copy in given:
        copy.wait()

    def phases(m, _):
        c = m // 14
        q = lax.rem(m, 14)
        index = (boost_ref[c] * (8 * i + q - 3)) & (NZ - 1)
        angle = jnp.full((8, 128), index, jnp.int32).astype(jnp.float32) * (2.0 * math.pi / NZ)
        trig[c, q, 0] = jnp.cos(angle)
        trig[c, q, 1] = jnp.sin(angle)
        return 0

    lax.fori_loop(0, 28, phases, 0)
    acc[...] = jnp.zeros_like(acc)
    p_buf[:, 0:24, :] = jnp.zeros((32, 24, 128), jnp.float32)
    p_buf[:, 88:112, :] = jnp.zeros((32, 24, 128), jnp.float32)

    pl.semaphore_wait(barrier, 6 + groups - 1)

    column = g // 8
    z_own = lax.rem(g, 8)

    def in_group(k):
        return lax.rem(g + k, groups)

    def in_column(k):
        return column * 8 + lax.rem(z_own + k, 8)

    def start(make, count):
        for k in sorted(range(1, count), key=lambda k: -min(k % 8, 8 - k % 8)):
            make(k).start()

    def wait_send(make, count):
        def body(k, _):
            make(k).wait_send()
            return 0
        lax.fori_loop(1, count, body, 0)

    def wait_recv(buf, sem, count, mine):
        def body(k, _):
            o = lax.rem(mine + k, count)
            pltpu.make_async_copy(buf.at[o], buf.at[o], sem.at[o]).wait()
            return 0
        lax.fori_loop(1, count, body, 0)

    def exchange(src, dst, send, recv, one, count, mine):
        def make(k):
            o = lax.rem(mine + k, count)
            to = in_group(k) if count == groups else in_column(k)
            return pltpu.make_async_remote_copy(
                src_ref=src if one else src.at[o], dst_ref=dst.at[mine], send_sem=send.at[o], recv_sem=recv.at[mine],
                device_id=(i, to), device_id_type=MESH)
        return make

    rs1_copy = exchange(d1, rs1, rs1_send, rs1_recv, False, 8, z_own)
    ag1_copy = exchange(sel1, ag1, ag1_send, ag1_recv, True, 8, z_own)
    rs2_copy = exchange(d2, rs2, rs2_send, rs2_recv, False, groups, g)
    ag2_copy = exchange(t2, ag2, ag2_send, ag2_recv, True, groups, g)

    def window(c, s, first, planes):
        return land.at[c, s, :, pl.ds(pl.multiple_of(first * 8, 8), planes * 8)]

    def move(slot, c, s, src, dst, planes, device):
        return pltpu.make_async_remote_copy(
            src_ref=window(c, s, src, planes), dst_ref=window(c, s, dst, planes),
            send_sem=slab_send.at[slot, c, s], recv_sem=slab_recv.at[slot, c, s],
            device_id=device, device_id_type=MESH)

    def far_copy(c, s):
        return move(TWO, c, s, 24 - 24 * c, 8 + 8 * c, 8, slab(2 - 4 * c))

    def last_copies():
        to = slab(2 - 4 * core), slab(4 * core - 2)
        return (move(TWO, 1 - core, 3, 24 * core, 16 - 8 * core, 8, to[1]),
                move(EDGE, core, 3, 30 - 30 * core, 14 + 2 * core, 2, to[0]),
                move(REST, core, 3, 24 - 22 * core, 8 + 10 * core, 6, to[0]))

    def near_copy(s):
        return move(ONE, core, s, 24 - 24 * core, 16 - 8 * core, 8, (mate, g))

    def third_copy(s):
        return move(THREE, 1 - core, s, 30 * core, 24 - 18 * core, 2, slab(6 * core - 3))

    def forward_one(s):
        return move(ONE, 1 - core, s, 16 - 8 * core, 8 + 8 * core, 8, (mate, g))

    def forward_three(s):
        return move(THREE, core, s, 14 + 2 * core, 6 + 18 * core, 2, (mate, g))

    def arrived(slot, c, s, planes):
        here = window(c, s, 0, planes)
        pltpu.make_async_copy(here, here, slab_recv.at[slot, c, s]).wait()

    def start_moves(s):
        for copy in last_copies() if s == 3 else (far_copy(0, s), far_copy(1, s)):
            copy.start()
        near_copy(s).start()
        third_copy(s).start()

    def forward(s):
        arrived(TWO, 0, s, 8)
        arrived(TWO, 1, s, 8)
        forward_one(s).start()
        forward_three(s).start()

    def forward_last():
        arrived(TWO, 1 - core, 3, 8)
        forward_one(3).start()
        arrived(EDGE, core, 3, 2)
        forward_three(3).start()

    start(rs1_copy, 8)
    for s in range(EARLY):
        start_moves(s)
    rs1[z_own] = d1[z_own]

    wait_recv(rs1, rs1_recv, 8, z_own)

    def add1(k, total):
        return total + rs1[k]

    t1[...] = lax.fori_loop(1, 8, add1, rs1[0])
    swap = pltpu.make_async_remote_copy(
        src_ref=t1, dst_ref=swapped, send_sem=swap_sem.at[0], recv_sem=swap_sem.at[1],
        device_id=peer(8), device_id_type=MESH)
    swap.start()
    for s in range(EARLY, SECOND):
        start_moves(s)
    swap.wait()
    t1[...] += swapped[...]

    def s1_copy(c, d):
        return pltpu.make_async_remote_copy(
            src_ref=t1.at[c], dst_ref=s1.at[c, d], send_sem=s1_send.at[c, d], recv_sem=s1_recv.at[c, d],
            device_id=slab((1 - 2 * c) * (d + 1)), device_id_type=MESH)

    cases = [(c, d) for c in range(2) for d in range(2)]
    for case in cases:
        s1_copy(*case).start()
    for s in range(SECOND, 4):
        start_moves(s)
    forward(0)
    for case in cases:
        s1_copy(*case).wait_recv()
    r0 = shift_ref[0] - 8
    r1 = shift_ref[1] - 8
    from_0 = ((z_own + r0) >> 3) & 1
    from_1 = ((7 - z_own + r1) >> 3) & 1
    sel1[0] = s1[0, from_0]
    sel1[1] = s1[1, from_1]
    start(ag1_copy, 8)
    ag1[z_own] = sel1[...]
    forward(1)
    wait_recv(ag1, ag1_recv, 8, z_own)

    def fields_now(p, _):
        n = kr = ki = None
        for c in range(2):
            src = (p - r0 if c == 0 else p + r1) & 7
            cos, sin = trig[c, p + 3, 0], trig[c, p + 3, 1]
            cos, sin = cos * cos - sin * sin, 2.0 * cos * sin
            a, b, e = ag1[src, c, 0], ag1[src, c, 1], ag1[src, c, 2]
            b, e = b * cos - e * sin, b * sin + e * cos
            n, kr, ki = (a, b, e) if c == 0 else (n + a, kr + b, ki + e)
        f0[0, p] = DT * (1.2 * two_thirds(n * (1.0 / STATES)) - 1.0)
        f0[1, p] = kr * (-3.0 * DT / STATES)
        f0[2, p] = ki * (-3.0 * DT / STATES)
        return 0

    lax.fori_loop(0, 8, fields_now, 0)

    tables = stencil_tables(0.5 * DT)

    def halo_copy(d, s):
        src = pl.ds(24, 24) if d == 0 else pl.ds(64, 24)
        dst = pl.ds(24, 24) if d == 0 else pl.ds(0, 24)
        vols = pl.ds(s * 8, 8)
        return pltpu.make_async_remote_copy(
            src_ref=p_buf.at[vols, src], dst_ref=h_buf.at[vols, dst],
            send_sem=halo_send.at[d, s], recv_sem=halo_recv.at[d, s],
            device_id=slab(2 * d - 1), device_id_type=MESH)

    def send_halos(s):
        halo_copy(0, s).start()
        halo_copy(1, s).start()

    def state_step(s, _):
        for c in range(2):
            arrived(ONE, c, s, 8)
            arrived(THREE, c, s, 2)
            for k in range(4):
                e_buf[k] = land[c, s, k, 48:208, :].reshape(20, 8, 128)
            vol = (s * 2 + c) * 4
            base = 7 - r0 if c == 0 else r1 - 1

            def boost(q, _):
                cos, sin = trig[c, q, 0], trig[c, q, 1]
                plane = jnp.maximum(jnp.minimum(base + q, 19), 0)
                ur, ui, vr, vi = (e_buf[k, plane] for k in range(4))
                to = pl.ds(pl.multiple_of(q * 8, 8), 8)
                b_buf[vol, to, :] = ur * cos - ui * sin
                b_buf[vol + 1, to, :] = ur * sin + ui * cos
                b_buf[vol + 2, to, :] = vr * cos + vi * sin
                b_buf[vol + 3, to, :] = vi * cos - vr * sin
                return 0

            lax.fori_loop(0, 14, boost, 0)

            def predict(m, _):
                p = m * M
                row = pl.multiple_of((p + 3) * 8, 8)
                pot, dr, di = (f0[q, pl.ds(p, M)] for q in range(3))
                ur, lur = laplacian(tables, b_buf, vol, row)
                ui, lui = laplacian(tables, b_buf, vol + 1, row)
                vr, lvr = laplacian(tables, b_buf, vol + 2, row)
                vi, lvi = laplacian(tables, b_buf, vol + 3, row)
                pur = ur - lui + (pot * ui + dr * vi + di * vr)
                pui = ui + lur - (pot * ur + dr * vr - di * vi)
                pvr = vr + lvi + (dr * ui - di * ur - pot * vi)
                pvi = vi - lvr - (dr * ur + di * ui - pot * vr)
                at = pl.ds(row, 8 * M)
                for k, v in enumerate((pur, pui, pvr, pvi)):
                    p_buf[vol + k, at, :] = v.reshape(8 * M, 128)
                acc[0, pl.ds(p, M)] += pvr * pvr + pvi * pvi
                acc[1, pl.ds(p, M)] += pur * pvr + pui * pvi
                acc[2, pl.ds(p, M)] += pui * pvr - pur * pvi
                return 0

            lax.fori_loop(0, 8 // M, predict, 0)

        @pl.when(s == 0)
        def _():
            forward(2)

        @pl.when(s == 1)
        def _():
            forward_last()

        @pl.when(s < 3)
        def _():
            send_halos(s)

        @pl.when(s == 2)
        def _():
            arrived(REST, core, 3, 6)

        return 0

    lax.fori_loop(0, 4, state_step, 0)

    for p in range(8):
        for q in range(3):
            v = acc[q, p]
            d2[p, q] = v[0:4]
            d2[8 + p, q] = v[4:8]

    start(rs2_copy, groups)
    send_halos(3)
    def kinetic_state(s, _):
        def kinetic(m, _):
            vol = (s * 2 + m // (8 // M)) * 4
            row = pl.multiple_of((lax.rem(m, 8 // M) * M + 3) * 8, 8)
            at = pl.ds(row, 8 * M)
            ur, lur = laplacian(tables, p_buf, vol, row)
            ui, lui = laplacian(tables, p_buf, vol + 1, row)
            vr, lvr = laplacian(tables, p_buf, vol + 2, row)
            vi, lvi = laplacian(tables, p_buf, vol + 3, row)
            for k, v in enumerate((ur - lui, ui + lur, vr + lvi, vi - lvr)):
                b_buf[vol + k, at, :] += v.reshape(8 * M, 128)
            return 0

        lax.fori_loop(0, 16 // M, kinetic, 0)
        return 0

    def edge_state(s, _):
        halo_copy(0, s).wait_recv()
        halo_copy(1, s).wait_recv()
        w1, w2, w3 = tables[0][1:]

        def edges(c, _):
            vol = (s * 2 + c) * 4
            for k, other, sign in ((0, 1, -1.0), (1, 0, 1.0), (2, 3, 1.0), (3, 2, -1.0)):
                for near, far in (((16, 8, 0), (24, 32, 40)), ((24, 32, 40), (80, 72, 64))):
                    h1, h2, h3 = (sign * h_buf[vol + other, row:row + 8, :] for row in near)
                    for row, v in zip(far, (w1 * h1 + w2 * h2 + w3 * h3, w2 * h1 + w3 * h2, w3 * h1)):
                        b_buf[vol + k, row:row + 8, :] += v
            return 0

        lax.fori_loop(0, 2, edges, 0)
        return 0

    rs2[g] = d2[g]
    lax.fori_loop(0, 3, kinetic_state, 0)
    wait_recv(rs2, rs2_recv, groups, g)

    def add2(k, total):
        return total + rs2[k]

    n, kr, ki = lax.fori_loop(1, groups, add2, rs2[0])
    t2[0] = DT * (1.2 * two_thirds(n * (1.0 / STATES)) - 1.0)
    t2[1] = kr * (-3.0 * DT / STATES)
    t2[2] = ki * (-3.0 * DT / STATES)
    start(ag2_copy, groups)
    ag2[g] = t2[...]

    lax.fori_loop(3, 4, kinetic_state, 0)
    lax.fori_loop(0, 4, edge_state, 0)

    def correct(t, _):
        p = (z_own + (1 - 2 * lax.rem(t, 2)) * ((t + 1) // 2) + 8) & 7
        for half in range(2):
            o = 8 * half + p

            @pl.when(o != g)
            def _():
                pltpu.make_async_copy(ag2.at[o], ag2.at[o], ag2_recv.at[o]).wait()

        pot, dr, di = (jnp.concatenate([ag2[p, q], ag2[8 + p, q]], axis=0) for q in range(3))
        at = pl.ds(pl.multiple_of((p + 3) * 8, 8), 8)
        to = pl.ds(p, 8, stride=8)
        for s in range(4):
            for c in range(2):
                vol = (s * 2 + c) * 4
                out = (c * 4 + s) * 4
                ur, ui, vr, vi = (p_buf[vol + k, at, :] for k in range(4))
                gur, gui, gvr, gvi = (b_buf[vol + k, at, :] for k in range(4))
                o_ref[out, to, :] = 0.5 * (gur + (pot * ui + dr * vi + di * vr))
                o_ref[out + 1, to, :] = 0.5 * (gui - (pot * ur + dr * vr - di * vi))
                o_ref[out + 2, to, :] = 0.5 * (gvr + (dr * ui - di * ur - pot * vi))
                o_ref[out + 3, to, :] = 0.5 * (gvi - (dr * ur + di * ui - pot * vr))
        return 0

    lax.fori_loop(0, 8, correct, 0)

    wait_send(rs1_copy, 8)
    wait_send(ag1_copy, 8)
    wait_send(rs2_copy, groups)
    wait_send(ag2_copy, groups)
    for case in cases:
        s1_copy(*case).wait_send()

    def moves_sent(s, _):
        for c in range(2):
            halo_copy(c, s).wait_send()
        near_copy(s).wait_send()
        third_copy(s).wait_send()
        forward_one(s).wait_send()
        forward_three(s).wait_send()
        return 0

    lax.fori_loop(0, 4, moves_sent, 0)
    for s in range(4):
        for copy in last_copies() if s == 3 else (far_copy(0, s), far_copy(1, s)):
            copy.wait_send()


def local(cloud_states, cloud_shift, boost_wave):
    f32 = jnp.float32
    hbm = pl.BlockSpec(memory_space=pltpu.HBM)
    operands = [pltpu.with_memory_space_constraint(a, pltpu.HBM) for a in (cloud_shift, boost_wave, cloud_states)]
    dma = pltpu.SemaphoreType.DMA
    out = pl.pallas_call(
        kernel,
        out_shape=jax.ShapeDtypeStruct((32, 64, 128), f32),
        in_specs=[hbm, hbm, hbm],
        out_specs=pl.BlockSpec(memory_space=pltpu.VMEM),
        scratch_shapes=[
            pltpu.SMEM((2,), jnp.int32),
            pltpu.SMEM((2,), jnp.int32),
            pltpu.VMEM((2, 4, 4, 8, 1024), f32),
            pltpu.VMEM((2, 4, 4, 256, 128), f32),
            pltpu.VMEM((4, 20, 8, 128), f32),
            pltpu.VMEM((32, 112, 128), f32),
            pltpu.VMEM((32, 112, 128), f32),
            pltpu.VMEM((32, 48, 128), f32),
            pltpu.VMEM((2, 14, 2, 8, 128), f32),
            pltpu.VMEM((8, 2, 3, 8, 128), f32),
            pltpu.VMEM((8, 2, 3, 8, 128), f32),
            pltpu.VMEM((2, 3, 8, 128), f32),
            pltpu.VMEM((2, 3, 8, 128), f32),
            pltpu.VMEM((2, 2, 3, 8, 128), f32),
            pltpu.VMEM((2, 3, 8, 128), f32),
            pltpu.VMEM((8, 2, 3, 8, 128), f32),
            pltpu.VMEM((3, 8, 8, 128), f32),
            pltpu.VMEM((3, 8, 8, 128), f32),
            pltpu.VMEM((16, 3, 4, 128), f32),
            pltpu.VMEM((16, 3, 4, 128), f32),
            pltpu.VMEM((3, 4, 128), f32),
            pltpu.VMEM((16, 3, 4, 128), f32),
            dma((4,)), dma((5, 2, 4)), dma((5, 2, 4)),
            dma((8,)), dma((8,)), dma((2,)), dma((2, 2)), dma((2, 2)), dma((8,)), dma((8,)),
            dma((16,)), dma((16,)), dma((16,)), dma((16,)), dma((2, 4)), dma((2, 4)),
        ],
        compiler_params=pltpu.CompilerParams(
            collective_id=0, has_side_effects=True, vmem_limit_bytes=VMEM_LIMIT),
    )(*operands)
    out = out.reshape(2, 4, 4, 8, 8, 128).transpose(0, 1, 2, 4, 3, 5)
    return out.reshape(2, 4, 4, 8, 1024)


def solution(mesh):
    in_specs = (P(None, "grp", None, "slab", None), P(), P())
    out_specs = P(None, "grp", None, "slab", None)
    return jax.shard_map(local, mesh=mesh, in_specs=in_specs, out_specs=out_specs, check_vma=False)
```

```python
import math

import jax
import jax.numpy as jnp
from jax import lax
from jax.experimental import pallas as pl
from jax.experimental.pallas import tpu as pltpu
from jax.sharding import PartitionSpec as P

MESH = pl.DeviceIdType.MESH
W = (-49.0 / 18.0, 1.5, -0.15, 1.0 / 90.0)
DT = 0.1
EARLY, SECOND = 1, 2
VMEM_LIMIT = 44 * 2**20
NZ = 128
STATES = 64
M = 8
ONE, THREE, TWO, EDGE, REST = range(5)


def stencil_tables(scale):
    lane = lax.broadcasted_iota(jnp.int32, (8, 128), 1)
    sub = lax.broadcasted_iota(jnp.int32, (8, 128), 0)
    y = lane % 32
    w = [scale * v for v in W]
    cy = {}
    for s in (1, -1, 2, -2, 3, -3):
        cy[s] = jnp.where((y + s >= 0) & (y + s < 32), w[abs(s)], 0.0)
    m32 = jnp.where(lane >= 32, w[1], w[3])
    m96 = jnp.where(lane < 96, w[1], w[3])
    up = [jnp.where((lane < 32 * j) & (sub < 7), w[j], 0.0) for j in (1, 2, 3)]
    down = [jnp.where((lane >= 128 - 32 * j) & (sub > 0), w[j], 0.0) for j in (1, 2, 3)]
    return w, cy, m32, m96, up, down


def laplacian(tables, ref, vol, row):
    w, cy, m32, m96, up, down = tables

    def plane(d):
        return ref[vol, pl.ds(pl.multiple_of(row + 8 * d, 8), 8 * M), :].reshape(M, 8, 128)

    f = plane(0)
    t = (3.0 * w[0]) * f
    for j in (1, 2, 3):
        t = t + w[j] * (plane(-j) + plane(j))
    for s in (1, -1, 2, -2, 3, -3):
        t = t + cy[s] * pltpu.roll(f, (-s) % 128, 2)
    r32, r64, r96 = (pltpu.roll(f, 32 * j, 2) for j in (1, 2, 3))
    t = t + m32 * r32 + w[2] * r64 + m96 * r96
    above = up[0] * r32 + up[1] * r64 + up[2] * r96
    below = down[0] * r96 + down[1] * r64 + down[2] * r32
    return f, t + pltpu.roll(above, 1, 1) + pltpu.roll(below, 7, 1)


def two_thirds(n):
    y = jnp.exp(jnp.log(jnp.maximum(n, 1e-30)) * (1.0 / 3.0))
    y = y - (y * y * y - n) / (3.0 * y * y)
    return y * y


def kernel(shift_in, boost_in, x_ref, o_ref,
           shift_ref, boost_ref, x_buf, land, e_buf, b_buf, p_buf, h_buf, trig, d1, rs1, t1, swapped, s1, sel1, ag1, f0, acc, d2, rs2, t2, ag2,
           x_sem, slab_send, slab_recv, rs1_send, rs1_recv, swap_sem, s1_send, s1_recv, ag1_send, ag1_recv,
           rs2_send, rs2_recv, ag2_send, ag2_recv, halo_send, halo_recv):
    slabs = lax.axis_size("slab")
    groups = lax.axis_size("grp")
    i = lax.axis_index("slab")
    g = lax.axis_index("grp")
    core = lax.rem(i, 2)
    mate = i + 1 - 2 * core

    def slab(d):
        return (lax.rem(i + d + slabs, slabs), g)

    def peer(k):
        return (i, lax.rem(g + k, groups))

    def own_copy(c):
        return pltpu.make_async_copy(x_ref.at[c], x_buf.at[c], x_sem.at[c])

    own_copy(0).start()
    own_copy(1).start()
    given = [pltpu.make_async_copy(a, b, x_sem.at[2 + n]) for n, (a, b) in enumerate(((shift_in, shift_ref), (boost_in, boost_ref)))]
    for copy in given:
        copy.start()

    barrier = pltpu.get_barrier_semaphore()
    for d in (1, -1, 2, -2, 3, -3):
        pl.semaphore_signal(barrier, inc=1, device_id=slab(d), device_id_type=MESH)

    def greet(k, _):
        pl.semaphore_signal(barrier, inc=1, device_id=peer(k), device_id_type=MESH)
        return 0

    lax.fori_loop(1, groups, greet, 0)

    for c in range(2):
        own_copy(c).wait()

        def relay(m, _):
            s = m // 4
            k = lax.rem(m, 4)
            for j in range(8):
                land[c, s, k, pl.ds(192 - 192 * c + j, 8, stride=8), :] = x_buf[c, s, k, :, 128 * j:128 * j + 128]
            return 0

        lax.fori_loop(0, 16, relay, 0)

        def terms(p, _):
            at = pl.ds(pl.multiple_of(192 - 192 * c + 8 * p, 8), 8)
            n = kr = ki = None
            for s in range(4):
                ur, ui, vr, vi = (land[c, s, k, at, :] for k in range(4))
                a = vr * vr + vi * vi
                b = ur * vr + ui * vi
                e = ui * vr - ur * vi
                n, kr, ki = (a, b, e) if s == 0 else (n + a, kr + b, ki + e)
            for q, v in enumerate((n, kr, ki)):
                d1[p, c, q] = v
            return 0

        lax.fori_loop(0, 8, terms, 0)

    pl.semaphore_wait(barrier, 6 + groups - 1)

    column = g // 8
    z_own = lax.rem(g, 8)

    def in_group(k):
        return lax.rem(g + k, groups)

    def in_column(k):
        return column * 8 + lax.rem(z_own + k, 8)

    def start(make, count):
        for k in sorted(range(1, count), key=lambda k: -min(k % 8, 8 - k % 8)):
            make(k).start()

    def wait_send(make, count):
        def body(k, _):
            make(k).wait_send()
            return 0
        lax.fori_loop(1, count, body, 0)

    def wait_recv(buf, sem, count, mine):
        for k in range(1, count):
            o = lax.rem(mine + k, count)
            pltpu.make_async_copy(buf.at[o], buf.at[o], sem.at[o]).wait()

    def exchange(src, dst, send, recv, one, count, mine):
        def make(k):
            o = lax.rem(mine + k, count)
            to = in_group(k) if count == groups else in_column(k)
            return pltpu.make_async_remote_copy(
                src_ref=src if one else src.at[o], dst_ref=dst.at[mine], send_sem=send.at[o], recv_sem=recv.at[mine],
                device_id=(i, to), device_id_type=MESH)
        return make

    rs1_copy = exchange(d1, rs1, rs1_send, rs1_recv, False, 8, z_own)
    ag1_copy = exchange(sel1, ag1, ag1_send, ag1_recv, True, 8, z_own)
    rs2_copy = exchange(d2, rs2, rs2_send, rs2_recv, False, groups, g)
    ag2_copy = exchange(t2, ag2, ag2_send, ag2_recv, True, groups, g)

    def window(c, s, first, planes):
        return land.at[c, s, :, pl.ds(pl.multiple_of(first * 8, 8), planes * 8)]

    def move(slot, c, s, src, dst, planes, device):
        return pltpu.make_async_remote_copy(
            src_ref=window(c, s, src, planes), dst_ref=window(c, s, dst, planes),
            send_sem=slab_send.at[slot, c, s], recv_sem=slab_recv.at[slot, c, s],
            device_id=device, device_id_type=MESH)

    def far_copy(c, s):
        return move(TWO, c, s, 24 - 24 * c, 8 + 8 * c, 8, slab(2 - 4 * c))

    def last_copies():
        to = slab(2 - 4 * core), slab(4 * core - 2)
        return (move(TWO, 1 - core, 3, 24 * core, 16 - 8 * core, 8, to[1]),
                move(EDGE, core, 3, 30 - 30 * core, 14 + 2 * core, 2, to[0]),
                move(REST, core, 3, 24 - 22 * core, 8 + 10 * core, 6, to[0]))

    def near_copy(s):
        return move(ONE, core, s, 24 - 24 * core, 16 - 8 * core, 8, (mate, g))

    def third_copy(s):
        return move(THREE, 1 - core, s, 30 * core, 24 - 18 * core, 2, slab(6 * core - 3))

    def forward_one(s):
        return move(ONE, 1 - core, s, 16 - 8 * core, 8 + 8 * core, 8, (mate, g))

    def forward_three(s):
        return move(THREE, core, s, 14 + 2 * core, 6 + 18 * core, 2, (mate, g))

    def arrived(slot, c, s, planes):
        here = window(c, s, 0, planes)
        pltpu.make_async_copy(here, here, slab_recv.at[slot, c, s]).wait()

    def start_moves(s):
        for copy in last_copies() if s == 3 else (far_copy(0, s), far_copy(1, s)):
            copy.start()
        near_copy(s).start()
        third_copy(s).start()

    def forward(s):
        arrived(TWO, 0, s, 8)
        arrived(TWO, 1, s, 8)
        forward_one(s).start()
        forward_three(s).start()

    def forward_last():
        arrived(TWO, 1 - core, 3, 8)
        forward_one(3).start()
        arrived(EDGE, core, 3, 2)
        forward_three(3).start()

    start(rs1_copy, 8)
    for s in range(EARLY):
        start_moves(s)
    rs1[z_own] = d1[z_own]

    for copy in given:
        copy.wait()

    def phases(m, _):
        c = m // 14
        q = lax.rem(m, 14)
        index = (boost_ref[c] * (8 * i + q - 3)) & (NZ - 1)
        angle = jnp.full((8, 128), index, jnp.int32).astype(jnp.float32) * (2.0 * math.pi / NZ)
        trig[c, q, 0] = jnp.cos(angle)
        trig[c, q, 1] = jnp.sin(angle)
        return 0

    lax.fori_loop(0, 28, phases, 0)
    acc[...] = jnp.zeros_like(acc)
    p_buf[:, 0:24, :] = jnp.zeros((32, 24, 128), jnp.float32)
    p_buf[:, 88:112, :] = jnp.zeros((32, 24, 128), jnp.float32)

    wait_recv(rs1, rs1_recv, 8, z_own)

    def add1(k, total):
        return total + rs1[k]

    t1[...] = lax.fori_loop(1, 8, add1, rs1[0])
    swap = pltpu.make_async_remote_copy(
        src_ref=t1, dst_ref=swapped, send_sem=swap_sem.at[0], recv_sem=swap_sem.at[1],
        device_id=peer(8), device_id_type=MESH)
    swap.start()
    for s in range(EARLY, SECOND):
        start_moves(s)
    swap.wait()
    t1[...] += swapped[...]

    def s1_copy(c, d):
        return pltpu.make_async_remote_copy(
            src_ref=t1.at[c], dst_ref=s1.at[c, d], send_sem=s1_send.at[c, d], recv_sem=s1_recv.at[c, d],
            device_id=slab((1 - 2 * c) * (d + 1)), device_id_type=MESH)

    cases = [(c, d) for c in range(2) for d in range(2)]
    for case in cases:
        s1_copy(*case).start()
    for s in range(SECOND, 4):
        start_moves(s)
    forward(0)
    for case in cases:
        s1_copy(*case).wait_recv()
    r0 = shift_ref[0] - 8
    r1 = shift_ref[1] - 8
    from_0 = ((z_own + r0) >> 3) & 1
    from_1 = ((7 - z_own + r1) >> 3) & 1
    sel1[0] = s1[0, from_0]
    sel1[1] = s1[1, from_1]
    start(ag1_copy, 8)
    ag1[z_own] = sel1[...]
    forward(1)
    wait_recv(ag1, ag1_recv, 8, z_own)

    def fields_now(p, _):
        n = kr = ki = None
        for c in range(2):
            src = (p - r0 if c == 0 else p + r1) & 7
            cos, sin = trig[c, p + 3, 0], trig[c, p + 3, 1]
            cos, sin = cos * cos - sin * sin, 2.0 * cos * sin
            a, b, e = ag1[src, c, 0], ag1[src, c, 1], ag1[src, c, 2]
            b, e = b * cos - e * sin, b * sin + e * cos
            n, kr, ki = (a, b, e) if c == 0 else (n + a, kr + b, ki + e)
        f0[0, p] = DT * (1.2 * two_thirds(n * (1.0 / STATES)) - 1.0)
        f0[1, p] = kr * (-3.0 * DT / STATES)
        f0[2, p] = ki * (-3.0 * DT / STATES)
        return 0

    lax.fori_loop(0, 8, fields_now, 0)

    tables = stencil_tables(0.5 * DT)

    def halo_copy(d, s):
        src = pl.ds(24, 24) if d == 0 else pl.ds(64, 24)
        dst = pl.ds(24, 24) if d == 0 else pl.ds(0, 24)
        vols = pl.ds(s * 8, 8)
        return pltpu.make_async_remote_copy(
            src_ref=p_buf.at[vols, src], dst_ref=h_buf.at[vols, dst],
            send_sem=halo_send.at[d, s], recv_sem=halo_recv.at[d, s],
            device_id=slab(2 * d - 1), device_id_type=MESH)

    def send_halos(s):
        halo_copy(0, s).start()
        halo_copy(1, s).start()

    def state_step(s, _):
        for c in range(2):
            arrived(ONE, c, s, 8)
            arrived(THREE, c, s, 2)
            for k in range(4):
                e_buf[k] = land[c, s, k, 48:208, :].reshape(20, 8, 128)
            vol = (s * 2 + c) * 4
            base = 7 - r0 if c == 0 else r1 - 1

            def boost(q, _):
                cos, sin = trig[c, q, 0], trig[c, q, 1]
                plane = jnp.maximum(jnp.minimum(base + q, 19), 0)
                ur, ui, vr, vi = (e_buf[k, plane] for k in range(4))
                to = pl.ds(pl.multiple_of(q * 8, 8), 8)
                b_buf[vol, to, :] = ur * cos - ui * sin
                b_buf[vol + 1, to, :] = ur * sin + ui * cos
                b_buf[vol + 2, to, :] = vr * cos + vi * sin
                b_buf[vol + 3, to, :] = vi * cos - vr * sin
                return 0

            lax.fori_loop(0, 14, boost, 0)

            def predict(m, _):
                p = m * M
                row = pl.multiple_of((p + 3) * 8, 8)
                pot, dr, di = (f0[q, pl.ds(p, M)] for q in range(3))
                ur, lur = laplacian(tables, b_buf, vol, row)
                ui, lui = laplacian(tables, b_buf, vol + 1, row)
                vr, lvr = laplacian(tables, b_buf, vol + 2, row)
                vi, lvi = laplacian(tables, b_buf, vol + 3, row)
                pur = ur - lui + (pot * ui + dr * vi + di * vr)
                pui = ui + lur - (pot * ur + dr * vr - di * vi)
                pvr = vr + lvi + (dr * ui - di * ur - pot * vi)
                pvi = vi - lvr - (dr * ur + di * ui - pot * vr)
                at = pl.ds(row, 8 * M)
                for k, v in enumerate((pur, pui, pvr, pvi)):
                    p_buf[vol + k, at, :] = v.reshape(8 * M, 128)
                acc[0, pl.ds(p, M)] += pvr * pvr + pvi * pvi
                acc[1, pl.ds(p, M)] += pur * pvr + pui * pvi
                acc[2, pl.ds(p, M)] += pui * pvr - pur * pvi
                return 0

            lax.fori_loop(0, 8 // M, predict, 0)

        @pl.when(s == 0)
        def _():
            forward(2)

        @pl.when(s == 1)
        def _():
            forward_last()

        @pl.when(s < 2)
        def _():
            send_halos(s)

        @pl.when(s == 2)
        def _():
            arrived(REST, core, 3, 6)

        return 0

    lax.fori_loop(0, 4, state_step, 0)

    for p in range(8):
        for q in range(3):
            v = acc[q, p]
            d2[p, q] = v[0:4]
            d2[8 + p, q] = v[4:8]

    start(rs2_copy, groups)
    send_halos(2)
    send_halos(3)
    def kinetic_state(s, _):
        def kinetic(m, _):
            vol = (s * 2 + m // (8 // M)) * 4
            row = pl.multiple_of((lax.rem(m, 8 // M) * M + 3) * 8, 8)
            at = pl.ds(row, 8 * M)
            ur, lur = laplacian(tables, p_buf, vol, row)
            ui, lui = laplacian(tables, p_buf, vol + 1, row)
            vr, lvr = laplacian(tables, p_buf, vol + 2, row)
            vi, lvi = laplacian(tables, p_buf, vol + 3, row)
            for k, v in enumerate((ur - lui, ui + lur, vr + lvi, vi - lvr)):
                b_buf[vol + k, at, :] += v.reshape(8 * M, 128)
            return 0

        lax.fori_loop(0, 16 // M, kinetic, 0)
        return 0

    def edge_state(s, _):
        halo_copy(0, s).wait_recv()
        halo_copy(1, s).wait_recv()
        w1, w2, w3 = tables[0][1:]

        def edges(c, _):
            vol = (s * 2 + c) * 4
            for k, other, sign in ((0, 1, -1.0), (1, 0, 1.0), (2, 3, 1.0), (3, 2, -1.0)):
                for near, far in (((16, 8, 0), (24, 32, 40)), ((24, 32, 40), (80, 72, 64))):
                    h1, h2, h3 = (sign * h_buf[vol + other, row:row + 8, :] for row in near)
                    for row, v in zip(far, (w1 * h1 + w2 * h2 + w3 * h3, w2 * h1 + w3 * h2, w3 * h1)):
                        b_buf[vol + k, row:row + 8, :] += v
            return 0

        lax.fori_loop(0, 2, edges, 0)
        return 0

    rs2[g] = d2[g]
    lax.fori_loop(0, 3, kinetic_state, 0)
    wait_recv(rs2, rs2_recv, groups, g)

    def add2(k, total):
        return total + rs2[k]

    n, kr, ki = lax.fori_loop(1, groups, add2, rs2[0])
    t2[0] = DT * (1.2 * two_thirds(n * (1.0 / STATES)) - 1.0)
    t2[1] = kr * (-3.0 * DT / STATES)
    t2[2] = ki * (-3.0 * DT / STATES)
    start(ag2_copy, groups)
    ag2[g] = t2[...]

    lax.fori_loop(3, 4, kinetic_state, 0)
    lax.fori_loop(0, 4, edge_state, 0)

    def correct(t, _):
        p = (z_own + (1 - 2 * lax.rem(t, 2)) * ((t + 1) // 2) + 8) & 7
        for half in range(2):
            o = 8 * half + p

            @pl.when(o != g)
            def _():
                pltpu.make_async_copy(ag2.at[o], ag2.at[o], ag2_recv.at[o]).wait()

        pot, dr, di = (jnp.concatenate([ag2[p, q], ag2[8 + p, q]], axis=0) for q in range(3))
        at = pl.ds(pl.multiple_of((p + 3) * 8, 8), 8)
        to = pl.ds(p, 8, stride=8)
        for s in range(4):
            for c in range(2):
                vol = (s * 2 + c) * 4
                out = (c * 4 + s) * 4
                ur, ui, vr, vi = (p_buf[vol + k, at, :] for k in range(4))
                gur, gui, gvr, gvi = (b_buf[vol + k, at, :] for k in range(4))
                o_ref[out, to, :] = 0.5 * (gur + (pot * ui + dr * vi + di * vr))
                o_ref[out + 1, to, :] = 0.5 * (gui - (pot * ur + dr * vr - di * vi))
                o_ref[out + 2, to, :] = 0.5 * (gvr + (dr * ui - di * ur - pot * vi))
                o_ref[out + 3, to, :] = 0.5 * (gvi - (dr * ur + di * ui - pot * vr))
        return 0

    lax.fori_loop(0, 8, correct, 0)

    wait_send(rs1_copy, 8)
    wait_send(ag1_copy, 8)
    wait_send(rs2_copy, groups)
    wait_send(ag2_copy, groups)
    for case in cases:
        s1_copy(*case).wait_send()

    def moves_sent(s, _):
        for c in range(2):
            halo_copy(c, s).wait_send()
        near_copy(s).wait_send()
        third_copy(s).wait_send()
        forward_one(s).wait_send()
        forward_three(s).wait_send()
        return 0

    lax.fori_loop(0, 4, moves_sent, 0)
    for s in range(4):
        for copy in last_copies() if s == 3 else (far_copy(0, s), far_copy(1, s)):
            copy.wait_send()


def local(cloud_states, cloud_shift, boost_wave):
    f32 = jnp.float32
    hbm = pl.BlockSpec(memory_space=pltpu.HBM)
    operands = [pltpu.with_memory_space_constraint(a, pltpu.HBM) for a in (cloud_shift, boost_wave, cloud_states)]
    dma = pltpu.SemaphoreType.DMA
    out = pl.pallas_call(
        kernel,
        out_shape=jax.ShapeDtypeStruct((32, 64, 128), f32),
        in_specs=[hbm, hbm, hbm],
        out_specs=pl.BlockSpec(memory_space=pltpu.VMEM),
        scratch_shapes=[
            pltpu.SMEM((2,), jnp.int32),
            pltpu.SMEM((2,), jnp.int32),
            pltpu.VMEM((2, 4, 4, 8, 1024), f32),
            pltpu.VMEM((2, 4, 4, 256, 128), f32),
            pltpu.VMEM((4, 20, 8, 128), f32),
            pltpu.VMEM((32, 112, 128), f32),
            pltpu.VMEM((32, 112, 128), f32),
            pltpu.VMEM((32, 48, 128), f32),
            pltpu.VMEM((2, 14, 2, 8, 128), f32),
            pltpu.VMEM((8, 2, 3, 8, 128), f32),
            pltpu.VMEM((8, 2, 3, 8, 128), f32),
            pltpu.VMEM((2, 3, 8, 128), f32),
            pltpu.VMEM((2, 3, 8, 128), f32),
            pltpu.VMEM((2, 2, 3, 8, 128), f32),
            pltpu.VMEM((2, 3, 8, 128), f32),
            pltpu.VMEM((8, 2, 3, 8, 128), f32),
            pltpu.VMEM((3, 8, 8, 128), f32),
            pltpu.VMEM((3, 8, 8, 128), f32),
            pltpu.VMEM((16, 3, 4, 128), f32),
            pltpu.VMEM((16, 3, 4, 128), f32),
            pltpu.VMEM((3, 4, 128), f32),
            pltpu.VMEM((16, 3, 4, 128), f32),
            dma((4,)), dma((5, 2, 4)), dma((5, 2, 4)),
            dma((8,)), dma((8,)), dma((2,)), dma((2, 2)), dma((2, 2)), dma((8,)), dma((8,)),
            dma((16,)), dma((16,)), dma((16,)), dma((16,)), dma((2, 4)), dma((2, 4)),
        ],
        compiler_params=pltpu.CompilerParams(
            collective_id=0, has_side_effects=True, vmem_limit_bytes=VMEM_LIMIT),
    )(*operands)
    out = out.reshape(2, 4, 4, 8, 8, 128).transpose(0, 1, 2, 4, 3, 5)
    return out.reshape(2, 4, 4, 8, 1024)


def solution(mesh):
    in_specs = (P(None, "grp", None, "slab", None), P(), P())
    out_specs = P(None, "grp", None, "slab", None)
    return jax.shard_map(local, mesh=mesh, in_specs=in_specs, out_specs=out_specs, check_vma=False)
```
